32 devices in a mesh: groups: 2 (over y), pool: 4 (over x, core), tp: 4 (over z).
Axes of the slice: x: 2, y: 2, z: 4, core: 2. Of those that a mesh axis runs over, the one named last changes fastest.
Arguments:
- queries: bfloat16 [192, 16384], P(('groups', 'pool', 'tp')), parts along dimension 0, may hold values from -6 to 6
- cached_entries: bfloat16 [192, 512, 512], P(('groups', 'pool', 'tp')), parts along dimension 0, may hold values from -4.5 to 4.5
- new_entry: bfloat16 [192, 512], P(('groups', 'pool', 'tp')), parts along dimension 0, may hold values from -4.5 to 4.5
- lengths: int32 [192], P(('groups', 'pool', 'tp')), parts along dimension 0, may hold values from 2 to 512, as said below
- residual: bfloat16 [192, 7168], P(('groups', 'pool'), 'tp'), parts along dimension 0, may hold values from -40 to 40
- out_weight: bfloat16 [16384, 7168], P('pool', 'tp'), may hold values from -0.046875 to 0.046875
- norm_gain: bfloat16 [7168], P('tp'), may hold values from 0.5 to 1.5
- gate_weight: bfloat16 [7168, 18432], P('tp', 'pool'), may hold values from -0.0625 to 0.0625
- up_weight: bfloat16 [7168, 18432], P('tp', 'pool'), may hold values from -0.0625 to 0.0625
- down_weight: bfloat16 [18432, 7168], P('pool', 'tp'), may hold values from -0.046875 to 0.046875
Outputs:
- layer_out: bfloat16 [192, 7168], P(('groups', 'pool'), 'tp'), parts along dimension 0
The draws below stay inside these ranges and needn't reach their ends.
There are 2 independent parts, one for each index of `groups`. The reference program is written for one: setup_inputs(seed, part) draws one part's arguments, and reference() takes and returns one part's arrays. A program takes and returns all parts, laid end to end along the dimension named above; an argument that names none is the same for every part. Nothing has to cross between parts.
Inputs may be any that keep to these rules, and one draw needn't show every extreme that they name: `lengths`: every request has at least 2 positions in use and at most 512; some request of every draw has exactly 512.
All inputs are finite; a program needn't handle non-finite values.
Results may differ from the reference program's by a relative error of at most 0.009.
Values may be sent and summed in bfloat16 or wider, within the bound.
A program may use at most 192 MiB of HBM per device.

```python
import math
import jax
import jax.numpy as jnp
from jax import lax

D = 7168
FF = 18432
HEADS = 64
HD = 256
L = 512
REQUESTS = 96


def draw_queries(key, part):
    base = jnp.clip(jax.random.normal(jax.random.fold_in(key, 22), (REQUESTS, HEADS, HD), jnp.float32), -4.5, 4.5)
    return base.reshape(REQUESTS, HEADS * HD).astype(jnp.bfloat16)


def draw_cached_entries(key, part):
    base = jnp.clip(jax.random.normal(jax.random.fold_in(key, 24), (REQUESTS, L, 2 * HD), jnp.float32), -4.5, 4.5)
    return base.astype(jnp.bfloat16)


def draw_lengths(key, part):
    drawn = jax.random.randint(jax.random.fold_in(key, 31), (REQUESTS,), 2, L + 1)
    full_at = jax.random.randint(jax.random.fold_in(key, 32), (), 0, REQUESTS)
    return jnp.where(jnp.arange(REQUESTS) == full_at, L, drawn).astype(jnp.int32)


def draw_residual(key, part):
    row_scale = 10.0 ** jax.random.uniform(jax.random.fold_in(key, 41), (REQUESTS, 1), jnp.float32)
    ramp = jnp.arange(D).astype(jnp.float32)[None, :] / D
    col_scale = 10.0 ** (0.5 * jax.random.uniform(jax.random.fold_in(key, 42), (1, D), jnp.float32) + 0.5 * ramp)
    base = jnp.clip(jax.random.normal(jax.random.fold_in(key, 44), (REQUESTS, D), jnp.float32), -4.0, 4.0)
    return (0.1 * base * row_scale * col_scale).astype(jnp.bfloat16)


def steps_of(stream_key, extent, shards, low, high):
    level = 1.0
    for position, parts in shards:
        heights = jax.random.uniform(jax.random.fold_in(jax.random.fold_in(stream_key, 6), position), (parts,), jnp.float32, low / len(shards), high / len(shards))
        level = level * jnp.repeat(jnp.exp(heights), extent[position] // parts).reshape((-1,) + (1,) * (len(extent) - 1 - position))
    return level


def bell_draw(rng, dims, spread, bound, pieces=(), kind=jnp.bfloat16):
    values = spread * jax.random.normal(rng, dims, jnp.float32)
    if pieces:
        values = values * steps_of(rng, dims, pieces, -0.22, 0.18)
    return jnp.clip(values, -bound, bound).astype(kind)


def setup_inputs(seed: int = 0, part: int = 0) -> dict:
    key_of = jax.random.split(jax.random.key(seed), 11)
    part_keys = jax.random.split(jax.random.fold_in(key_of[10], part), 11)
    queries = draw_queries(jax.random.fold_in(jax.random.fold_in(key_of[10], part), 71), part)
    cached_entries = draw_cached_entries(jax.random.fold_in(jax.random.fold_in(key_of[10], part), 71), part)
    new_entry = bell_draw(part_keys[2], (REQUESTS, 2 * HD), 1.0, 4.5, ((0, 16),))
    lengths = draw_lengths(jax.random.fold_in(jax.random.fold_in(key_of[10], part), 71), part)
    residual = draw_residual(jax.random.fold_in(jax.random.fold_in(key_of[10], part), 71), part)
    out_weight = bell_draw(key_of[5], (HEADS * HD, D), (HEADS * HD) ** -0.5, 0.046875, ((0, 4), (1, 4)))
    norm_gain = jnp.clip(1.0 + 0.1 * jax.random.normal(key_of[6], (D,), jnp.float32), 0.5, 1.5).astype(jnp.bfloat16)
    gate_weight = bell_draw(key_of[7], (D, FF), D ** -0.5, 0.0625, ((0, 4), (1, 4)))
    up_weight = bell_draw(key_of[8], (D, FF), D ** -0.5, 0.0625, ((0, 4), (1, 4)))
    down_weight = bell_draw(key_of[9], (FF, D), FF ** -0.5, 0.046875, ((0, 4), (1, 4)))
    return {"queries": queries, "cached_entries": cached_entries, "new_entry": new_entry, "lengths": lengths, "residual": residual, "out_weight": out_weight, "norm_gain": norm_gain, "gate_weight": gate_weight, "up_weight": up_weight, "down_weight": down_weight}


def attend_one(query_row, entry_rows, new_row, length):
    query_heads = query_row.astype(jnp.float32).reshape(HEADS, HD)
    key_rows = entry_rows[:, :HD].astype(jnp.float32)
    value_rows = entry_rows[:, HD:].astype(jnp.float32)
    factor = 1.0 / math.sqrt(HD)
    scores = jnp.dot(query_heads, key_rows.T) * factor
    own_score = jnp.dot(query_heads, new_row[:HD].astype(jnp.float32)) * factor
    usable = jnp.arange(L) < length
    scores = jnp.where(usable[None, :], scores, -jnp.inf)
    peak_score = jnp.maximum(lax.optimization_barrier(jnp.max(scores, axis=1)), own_score)
    weights_raw = jnp.where(usable[None, :], jnp.exp(scores - peak_score[:, None]), 0.0)
    own_raw = jnp.exp(own_score - peak_score)
    totals = lax.optimization_barrier(jnp.sum(weights_raw, axis=1)) + own_raw
    weights = lax.optimization_barrier((weights_raw / totals[:, None]).astype(jnp.bfloat16)).astype(jnp.float32)
    own_weight = lax.optimization_barrier((own_raw / totals).astype(jnp.bfloat16)).astype(jnp.float32)
    mixture = jnp.dot(weights, value_rows) + own_weight[:, None] * new_row[HD:].astype(jnp.float32)[None, :]
    return mixture.reshape(HEADS * HD).astype(jnp.bfloat16)

def reference(queries, cached_entries, new_entry, lengths, residual, out_weight, norm_gain, gate_weight, up_weight, down_weight):
    attended = lax.map(lambda items: attend_one(items[0], items[1], items[2], items[3]), (queries, cached_entries, new_entry, lengths))
    post_attn = jnp.dot(attended, out_weight, preferred_element_type=jnp.float32) + residual.astype(jnp.float32)
    scaled = (post_attn * norm_gain.astype(jnp.float32)[None, :]).astype(jnp.bfloat16)
    inv_rms = lax.rsqrt(lax.optimization_barrier(jnp.mean(post_attn * post_attn, axis=1)) + 1e-06)
    gate_pre = jnp.dot(scaled, gate_weight, preferred_element_type=jnp.float32) * inv_rms[:, None]
    up_pre = jnp.dot(scaled, up_weight, preferred_element_type=jnp.float32) * inv_rms[:, None]
    hidden = (jax.nn.silu(gate_pre) * up_pre).astype(jnp.bfloat16)
    return (post_attn + jnp.dot(hidden, down_weight, preferred_element_type=jnp.float32)).astype(jnp.bfloat16)
```

```python
import functools
import math
import types

import jax
import jax.numpy as jnp
import numpy as np
from jax import lax
from jax.experimental import pallas as pl
from jax.experimental.pallas import tpu as pltpu
from jax.sharding import PartitionSpec as P

D = 7168
HEADS = 64
HD = 256


epsilon = 1e-06


def attend(queries, cached_entries, new_entry, lengths):
    amount = queries.shape[0]
    query_heads = queries.reshape(amount, HEADS, HD)
    key_rows = cached_entries[:, :, :HD]
    value_rows = cached_entries[:, :, HD:]
    factor = 1.0 / math.sqrt(HD)
    scores = (
        jnp.einsum("rhd,rld->rhl", query_heads, key_rows, preferred_element_type=jnp.float32)
        * factor
    )
    own_score = (
        jnp.einsum("rhd,rd->rh", query_heads, new_entry[:, :HD], preferred_element_type=jnp.float32)
        * factor
    )
    positions = lax.broadcasted_iota(jnp.int32, scores.shape, 2)
    usable = positions < lengths[:, None, None]
    scores = jnp.where(usable, scores, -jnp.inf)
    peak_score = jnp.maximum(jnp.max(scores, axis=2), own_score)
    weights_raw = jnp.where(usable, jnp.exp(scores - peak_score[:, :, None]), 0.0)
    own_raw = jnp.exp(own_score - peak_score)
    totals = jnp.sum(weights_raw, axis=2) + own_raw
    weights = (weights_raw / totals[:, :, None]).astype(jnp.bfloat16)
    own_weight = (own_raw / totals).astype(jnp.bfloat16)
    mixture = jnp.einsum("rhl,rld->rhd", weights, value_rows, preferred_element_type=jnp.float32)
    mixture = mixture + own_weight.astype(jnp.float32)[:, :, None] * new_entry[:, None, HD:].astype(
        jnp.float32
    )
    return mixture.reshape(amount, HEADS * HD).astype(jnp.bfloat16)


PAD = 8
LAG = 3
BACK_LAG = 3
SLOTS = 8
CHUNKS = 4
MESH = pl.DeviceIdType.MESH


def tile_of(extent):
    return 256 if extent % 256 == 0 else 128


def sizes_of(pools, tps, amount, block, width, cols, ff):
    rows = block * pools
    wide = 256 if ff % 256 == 0 else 384
    parts = 2 if width % 256 == 0 else 1
    pieces = ff // wide
    return types.SimpleNamespace(
        pools=pools,
        tps=tps,
        chips=pools // 2,
        amount=amount,
        block=block,
        width=width,
        cols=cols,
        ff=ff,
        rows=rows,
        half=rows // 2,
        slab=pools * amount,
        chunk=cols // CHUNKS,
        parts=parts,
        part=width // parts,
        wide=wide,
        low=(wide // 256 * 128 if wide % 256 == 0 else 256, 128),
        pieces=pieces,
        group=2 if pieces % 2 == 0 else 1,
        slots=min(SLOTS, pieces),
        lanes=-(-rows // 128) * 128,
        out_tile=width // parts if rows <= 256 else tile_of(width // parts),
    )


def scratch_of(z):
    bf16, f32 = jnp.bfloat16, jnp.float32
    dma = pltpu.SemaphoreType.DMA
    vmem = pltpu.VMEM
    held = {
        "wo": vmem((z.cols, z.width), bf16),
        "wgu": vmem((z.slots, z.width, 2 * z.wide), bf16),
        "wd": vmem((z.ff, z.width), bf16),
        "raw": vmem((z.pools, PAD, z.cols), bf16),
        "slabs": vmem((z.tps, CHUNKS, z.slab, z.chunk), bf16),
        "x": vmem((z.rows, z.chunk), bf16),
        "pf": vmem((z.rows, z.width), f32),
        "pair_out": vmem((z.parts, z.half, z.part), bf16),
        "pair_in": vmem((z.parts, z.half, z.part), bf16),
        "chip_out": vmem((z.parts, z.half, z.part), bf16),
        "chip_in": vmem((z.chips, z.parts, z.half, z.part), bf16),
        "post": vmem((z.half, z.width), f32),
        "own_post": vmem((z.block, z.width), f32),
        "s_in": vmem((z.rows, z.width), bf16),
        "sq_half": vmem((8, z.lanes), f32),
        "sq_pair": vmem((8, z.lanes), f32),
        "sq_all": vmem((z.tps, 8, z.lanes), f32),
        "inv": vmem((z.rows, 128), f32),
        "sums": vmem((z.pieces, z.rows, 2 * z.wide), f32),
        "acc": vmem((z.rows, z.width), f32),
        "end_out": vmem((z.parts, z.half, z.part), bf16),
        "end_in": vmem((z.parts, z.half, z.part), bf16),
        "last_out": vmem((z.chips, z.parts, z.block, z.part), bf16),
        "last_in": vmem((z.chips, z.parts, z.block, z.part), bf16),
        "wo_sem": dma((CHUNKS,)),
        "wd_sem": dma((1,)),
        "g_sem": dma((z.slots,)),
        "u_sem": dma((z.slots,)),
        "a_send": dma((CHUNKS, z.pools)),
        "a_recv": dma((CHUNKS, z.pools)),
        "c_right": dma((z.tps, CHUNKS)),
        "c_left": dma((z.tps, CHUNKS)),
        "c_recv": dma((z.tps, CHUNKS)),
        "pair_send": dma((z.parts,)),
        "pair_recv": dma((z.parts,)),
        "chip_send": dma((z.chips, z.parts)),
        "chip_recv": dma((z.chips, z.parts)),
        "in_send": dma((z.parts,)),
        "in_recv": dma((z.parts,)),
        "sq_send": dma((1,)),
        "sq_recv": dma((1,)),
        "end_send": dma((z.parts,)),
        "end_recv": dma((z.parts,)),
        "last_send": dma((z.chips, z.parts)),
        "last_recv": dma((z.chips, z.parts)),
        "e_send": dma((2,)),
        "e_recv": dma((z.tps,)),
    }
    for s in range(2):
        held["sbuf%d" % s] = vmem((z.pieces, z.rows, 2 * z.low[s]), bf16)
        held["rbuf%d" % s] = vmem((z.pieces, z.rows, 2 * z.low[s]), bf16)
        held["hid%d" % s] = vmem((z.pieces, z.rows, z.low[s]), bf16)
        for name in ("r_send", "r_recv", "h_send", "h_recv"):
            held["%s%d" % (name, s)] = dma((z.pieces,))
    return held


def layer_kernel(z, names, att, resid, gain, pick_local, pick_all, wo_hbm, wg_hbm, wu_hbm, wd_hbm, out, *refs):
    v = types.SimpleNamespace(**dict(zip(names, refs)))
    bf16, f32 = jnp.bfloat16, jnp.float32
    p = lax.axis_index("pool")
    t = lax.axis_index("tp")
    core, chip = lax.rem(p, 2), p // 2
    partner = p + 1 - 2 * core
    last = z.tps - 1
    before, behind = lax.rem(t + z.tps - 1, z.tps), lax.rem(t + 1, z.tps)
    mine = pl.ds(pl.multiple_of(core * z.half, 16), z.half)
    other = pl.ds(pl.multiple_of((1 - core) * z.half, 16), z.half)
    block_in_half = pl.ds(pl.multiple_of(chip * z.block, 8), z.block)
    low_at = (0, z.low[0])

    def span(j, extent):
        return pl.ds(pl.multiple_of(j * extent, 128), extent)

    def wo_copy(k):
        at = pl.ds(pl.multiple_of(k * z.chunk, 128), z.chunk)
        return pltpu.make_async_copy(wo_hbm.at[at], v.wo.at[at], v.wo_sem.at[k])

    def weight_copies(j):
        slot = lax.rem(j, z.slots)
        at = span(j, z.wide)
        return (
            pltpu.make_async_copy(wg_hbm.at[:, at], v.wgu.at[slot, :, pl.ds(0, z.wide)], v.g_sem.at[slot]),
            pltpu.make_async_copy(wu_hbm.at[:, at], v.wgu.at[slot, :, pl.ds(z.wide, z.wide)], v.u_sem.at[slot]),
        )

    wd_copy = pltpu.make_async_copy(wd_hbm, v.wd, v.wd_sem.at[0])

    def remote(src, dst, send, recv, device):
        return pltpu.make_async_remote_copy(
            src_ref=src, dst_ref=dst, send_sem=send, recv_sem=recv, device_id=device, device_id_type=MESH
        )

    for k in range(CHUNKS):
        wo_copy(k).start()

    barrier = pltpu.get_barrier_semaphore()
    for k in range(1, z.pools):
        pl.semaphore_signal(barrier, inc=1, device_id={"pool": lax.rem(p + k, z.pools)}, device_id_type=MESH)
    for k in range(1, z.tps):
        pl.semaphore_signal(barrier, inc=1, device_id={"tp": lax.rem(t + k, z.tps)}, device_id_type=MESH)
    pl.semaphore_wait(barrier, z.pools + z.tps - 2)

    def att_copy(j, k):
        q = lax.rem(p + j, z.pools)
        at = pl.ds(k * z.chunk, z.chunk)
        return remote(att.at[q, :, at], v.raw.at[p, :, at], v.a_send.at[k, j], v.a_recv.at[k, p], {"pool": q})

    def att_arrival(j, k):
        q = lax.rem(p + j, z.pools)
        at = pl.ds(k * z.chunk, z.chunk)
        return remote(att.at[q, :, at], v.raw.at[q, :, at], v.a_send.at[k, j], v.a_recv.at[k, q], {"pool": q})

    for k in range(CHUNKS):
        for j in range(1, z.pools):
            att_copy(j, k).start()
    for j in range(z.slots):
        for copy in weight_copies(jnp.int32(j)):
            copy.start()
    wd_copy.start()
    v.raw[p] = att[p]
    v.pf[...] = jnp.zeros_like(v.pf)

    def slab_right(origin, k):
        ref = v.slabs.at[origin, k]
        return remote(ref, ref, v.c_right.at[origin, k], v.c_recv.at[origin, k], {"tp": behind})

    def slab_left(origin, k):
        ref = v.slabs.at[origin, k]
        return remote(ref, ref, v.c_left.at[origin, k], v.c_recv.at[origin, k], {"tp": before})

    for k in range(CHUNKS):
        for j in range(1, z.pools):
            att_arrival(j, k).wait_recv()
        tall = jnp.concatenate([v.raw[q, :, pl.ds(k * z.chunk, z.chunk)].astype(f32) for q in range(z.pools)], axis=0)
        v.slabs[t, k] = jnp.dot(pick_local[...], tall.astype(bf16), preferred_element_type=f32).astype(bf16)

        @pl.when(t < last)
        def _():
            slab_right(t, k).start()

        @pl.when(t > 0)
        def _():
            slab_left(t, k).start()

    def gather_step(d, k):
        @pl.when(t - d >= 0)
        def _():
            slab_left(t - d, k).wait_recv()

            @pl.when(t < last)
            def _():
                slab_right(t - d, k).start()

        @pl.when(t + d <= last)
        def _():
            slab_right(t + d, k).wait_recv()

            @pl.when(t > 0)
            def _():
                slab_left(t + d, k).start()

    for d in range(1, last):
        pl.loop(0, CHUNKS)(functools.partial(gather_step, d))

    def rows_of(k):
        gather_step(last, k)
        tall = jnp.concatenate([v.slabs[o, k].astype(f32) for o in range(z.tps)], axis=0)
        v.x[...] = jnp.dot(pick_all[...], tall.astype(bf16), preferred_element_type=f32).astype(bf16)
        wo_copy(k).wait()

    def project(k, at):
        down_rows = pl.ds(pl.multiple_of(k * z.chunk, 128), z.chunk)
        v.pf[:, at] += jnp.dot(v.x[...], v.wo[down_rows, at], preferred_element_type=f32)

    @pl.loop(0, CHUNKS - 1)
    def _(k):
        rows_of(k)

        @pl.loop(0, z.width // z.out_tile)
        def _(n):
            project(k, span(n, z.out_tile))

    def pair_copy(n):
        return remote(
            v.pair_out.at[n], v.pair_in.at[n], v.pair_send.at[n], v.pair_recv.at[n], {"pool": partner}
        )

    def chip_copy(j, n):
        to = lax.rem(chip + j, z.chips)
        return remote(
            v.chip_out.at[n], v.chip_in.at[chip, n], v.chip_send.at[j, n], v.chip_recv.at[chip, n], {"pool": 2 * to + core}
        )

    def chip_arrival(j, n):
        to = lax.rem(chip + j, z.chips)
        return remote(
            v.chip_out.at[n], v.chip_in.at[to, n], v.chip_send.at[j, n], v.chip_recv.at[to, n], {"pool": 2 * to + core}
        )

    def in_copy(n):
        ref = v.s_in.at[mine, pl.ds(n * z.part, z.part)]
        return remote(ref, ref, v.in_send.at[n], v.in_recv.at[n], {"pool": partner})

    def in_arrival(n):
        ref = v.s_in.at[other, pl.ds(n * z.part, z.part)]
        return remote(ref, ref, v.in_send.at[n], v.in_recv.at[n], {"pool": partner})

    sq_copy = remote(v.sq_half, v.sq_pair, v.sq_send.at[0], v.sq_recv.at[0], {"pool": partner})

    rows_of(CHUNKS - 1)
    for n in range(z.parts):
        at = pl.ds(n * z.part, z.part)

        @pl.loop(0, z.part // z.out_tile)
        def _(m):
            project(CHUNKS - 1, pl.ds(pl.multiple_of(n * z.part + m * z.out_tile, 128), z.out_tile))

        v.pair_out[n] = v.pf[other, at].astype(bf16)
        pair_copy(n).start()

    for n in range(z.parts):
        at = pl.ds(n * z.part, z.part)
        pair_copy(n).wait_recv()
        v.post[:, at] = v.pf[mine, at] + v.pair_in[n].astype(f32)
        v.post[block_in_half, at] += resid[:, at].astype(f32)
        v.chip_out[n] = v.post[:, at].astype(bf16)
        for j in range(1, z.chips):
            chip_copy(j, n).start()

    squares = jnp.zeros((z.half, 1), f32)
    for n in range(z.parts):
        at = pl.ds(n * z.part, z.part)
        value = v.post[:, at]
        for j in range(1, z.chips):
            chip_arrival(j, n).wait_recv()
            value = value + v.chip_in[lax.rem(chip + j, z.chips), n].astype(f32)
        v.post[:, at] = value
        v.s_in[mine, at] = (value * gain[:, at]).astype(bf16)
        in_copy(n).start()
        squares = squares + jnp.sum(value * value, axis=1, keepdims=True)

    lane = lax.broadcasted_iota(jnp.int32, (z.half, z.lanes), 1)
    row = lax.broadcasted_iota(jnp.int32, (z.half, z.lanes), 0) + core * z.half
    flat = jnp.sum(jnp.where(lane == row, squares, 0.0), axis=0, keepdims=True)
    v.sq_half[...] = jnp.broadcast_to(flat, (8, z.lanes))
    sq_copy.start()
    v.own_post[...] = v.post[block_in_half, :]
    v.acc[...] = jnp.zeros_like(v.acc)
    for n in range(z.parts):
        in_arrival(n).wait_recv()
    sq_copy.wait_recv()
    v.sq_all[t] = v.sq_half[...] + v.sq_pair[...]

    ends = (0, last)

    def square_copy(s):
        return remote(v.sq_all.at[t], v.sq_all.at[t], v.e_send.at[s], v.e_recv.at[t], {"tp": ends[s]})

    def square_arrival(o):
        return remote(v.sq_all.at[o], v.sq_all.at[o], v.e_send.at[0], v.e_recv.at[o], {"tp": o})

    for s in range(2):

        @pl.when(t != ends[s])
        def _():
            square_copy(s).start()

    def scale_rows():
        for o in range(z.tps):

            @pl.when(t != o)
            def _():
                square_arrival(o).wait_recv()

        total = v.sq_all[0]
        for o in range(1, z.tps):
            total = total + v.sq_all[o]
        lane = lax.broadcasted_iota(jnp.int32, (z.rows, z.lanes), 1)
        row = lax.broadcasted_iota(jnp.int32, (z.rows, z.lanes), 0)
        tall = jnp.sum(jnp.where(lane == row, total[0:1], 0.0), axis=1, keepdims=True)
        v.inv[...] = jnp.broadcast_to(lax.rsqrt(tall / D + epsilon), (z.rows, 128))

    hid = (v.hid0, v.hid1)
    sbuf, rbuf = (v.sbuf0, v.sbuf1), (v.rbuf0, v.rbuf1)
    r_send, r_recv = (v.r_send0, v.r_send1), (v.r_recv0, v.r_recv1)
    h_send, h_recv = (v.h_send0, v.h_send1), (v.h_recv0, v.h_recv1)

    def lanes(s):
        if s == 0:
            return last - t, before, behind
        return t, behind, before

    def sum_hop(s, j):
        return remote(sbuf[s].at[j], rbuf[s].at[j], r_send[s].at[j], r_recv[s].at[j], {"tp": lanes(s)[1]})

    def hidden_hop(s, j):
        return remote(hid[s].at[j], hid[s].at[j], h_send[s].at[j], h_recv[s].at[j], {"tp": lanes(s)[2]})

    def compute(j):
        for copy in weight_copies(j):
            copy.wait()
        v.sums[j] = jnp.dot(v.s_in[...], v.wgu[lax.rem(j, z.slots)], preferred_element_type=f32)

        @pl.when(j + z.slots < z.pieces)
        def _():
            for copy in weight_copies(j + z.slots):
                copy.start()

    def down(g, at):
        held = [hid[s][g * z.group + b] for b in range(z.group) for s in range(2)]
        extent = z.group * z.wide
        v.acc[:, at] += jnp.dot(
            jnp.concatenate(held, axis=1),
            v.wd[pl.ds(pl.multiple_of(g * extent, 128), extent), at],
            preferred_element_type=f32,
        )

    wd_copy.wait()
    compute(jnp.int32(0))
    groups = z.pieces // z.group

    def one_step(i):
        for s in range(2):
            far, _, _ = lanes(s)
            c = i - LAG * far
            at_gate = pl.ds(low_at[s], z.low[s])
            at_up = pl.ds(z.wide + low_at[s], z.low[s])

            @pl.when((c >= 0) & (c < z.pieces))
            def _():
                @pl.when(far > 0)
                def _():
                    sum_hop(s, c).wait_recv()
                    v.sums[c, :, at_gate] += rbuf[s][c, :, : z.low[s]].astype(f32)
                    v.sums[c, :, at_up] += rbuf[s][c, :, z.low[s] :].astype(f32)

                @pl.when(far < last)
                def _():
                    sbuf[s][c, :, : z.low[s]] = v.sums[c, :, at_gate].astype(bf16)
                    sbuf[s][c, :, z.low[s] :] = v.sums[c, :, at_up].astype(bf16)
                    sum_hop(s, c).start()

                @pl.when(far == last)
                def _():
                    @pl.when(c == 0)
                    def _():
                        scale_rows()

                    inv = v.inv[:, :1]
                    gate = v.sums[c, :, at_gate] * inv
                    up = v.sums[c, :, at_up] * inv
                    hid[s][c] = (gate / (1.0 + jnp.exp(-gate)) * up).astype(bf16)
                    hidden_hop(s, c).start()

        for s in range(2):
            far, _, _ = lanes(s)
            back = last - far
            c = i - LAG * last - BACK_LAG * back

            @pl.when((back > 0) & (c >= 0) & (c < z.pieces))
            def _():
                hidden_hop(s, c).wait_recv()

                @pl.when(back < last)
                def _():
                    hidden_hop(s, c).start()

        @pl.when(i + 1 < z.pieces)
        def _():
            compute(i + 1)

        c = i - LAG * last - BACK_LAG * jnp.maximum(t, last - t)
        g = lax.div(c, z.group)

        @pl.when((c >= 0) & (lax.rem(c, z.group) == z.group - 1) & (g < groups - 1))
        def _():
            @pl.loop(0, z.width // z.out_tile)
            def _(n):
                down(g, span(n, z.out_tile))

    pl.loop(0, z.pieces + (LAG + BACK_LAG) * last)(one_step)

    def end_copy(n):
        return remote(v.end_out.at[n], v.end_in.at[n], v.end_send.at[n], v.end_recv.at[n], {"pool": partner})

    def last_copy(j, n):
        to = lax.rem(chip + j, z.chips)
        return remote(
            v.last_out.at[to, n], v.last_in.at[chip, n], v.last_send.at[j, n], v.last_recv.at[chip, n], {"pool": 2 * to + core}
        )

    def last_arrival(j, n):
        to = lax.rem(chip + j, z.chips)
        return remote(
            v.last_out.at[to, n], v.last_in.at[to, n], v.last_send.at[j, n], v.last_recv.at[to, n], {"pool": 2 * to + core}
        )

    for n in range(z.parts):

        @pl.loop(0, z.part // z.out_tile)
        def _(m):
            down(groups - 1, pl.ds(pl.multiple_of(n * z.part + m * z.out_tile, 128), z.out_tile))

        v.end_out[n] = v.acc[other, pl.ds(n * z.part, z.part)].astype(bf16)
        end_copy(n).start()
    for n in range(z.parts):
        at = pl.ds(n * z.part, z.part)
        end_copy(n).wait_recv()
        v.post[:, at] = v.acc[mine, at] + v.end_in[n].astype(f32)
        for q in range(z.chips):
            v.last_out[q, n] = v.post[pl.ds(q * z.block, z.block), at].astype(bf16)
        for j in range(1, z.chips):
            last_copy(j, n).start()
    for n in range(z.parts):
        at = pl.ds(n * z.part, z.part)
        total = v.own_post[:, at] + v.post[block_in_half, at]
        for j in range(1, z.chips):
            last_arrival(j, n).wait_recv()
            total = total + v.last_in[lax.rem(chip + j, z.chips), n].astype(f32)
        out[:, at] = total.astype(bf16)

    for j in range(1, z.pools):
        for k in range(CHUNKS):
            att_copy(j, k).wait_send()
    for n in range(z.parts):
        pair_copy(n).wait_send()
        in_copy(n).wait_send()
        end_copy(n).wait_send()
        for j in range(1, z.chips):
            chip_copy(j, n).wait_send()
            last_copy(j, n).wait_send()
    sq_copy.wait_send()
    for s in range(2):

        @pl.when(t != ends[s])
        def _():
            square_copy(s).wait_send()

    @pl.loop(0, CHUNKS)
    def _(k):
        for origin in range(z.tps):

            @pl.when((t < last) & (origin <= t))
            def _():
                slab_right(origin, k).wait_send()

            @pl.when((t > 0) & (origin >= t))
            def _():
                slab_left(origin, k).wait_send()

    @pl.loop(0, z.pieces)
    def _(c):
        for s in range(2):
            far, _, _ = lanes(s)

            @pl.when(far < last)
            def _():
                sum_hop(s, c).wait_send()

            @pl.when(far > 0)
            def _():
                hidden_hop(s, c).wait_send()


def finish_rows(att, resid, gain, out_weight, gate_weight, up_weight, down_weight, amount):
    pools, tps = lax.axis_size("pool"), lax.axis_size("tp")
    block, width = resid.shape
    z = sizes_of(pools, tps, amount, block, width, att.shape[2], gate_weight.shape[1])

    local = np.arange(z.slab)
    pick_local = np.zeros((z.slab, pools * PAD), np.float32)
    pick_local[local, local // amount * PAD + local % amount] = 1
    every = np.arange(z.rows)
    of_core, of_chip = every // z.half, every % z.half // block
    of_tp, of_row = every // amount % tps, every % amount
    pick_all = np.zeros((z.rows, z.rows), np.float32)
    pick_all[every, (of_tp * pools + 2 * of_chip + of_core) * amount + of_row] = 1

    vmem = pl.BlockSpec(memory_space=pltpu.VMEM)
    anywhere = pl.BlockSpec(memory_space=pl.ANY)
    bf16 = jnp.bfloat16
    held = scratch_of(z)
    return pl.pallas_call(
        functools.partial(layer_kernel, z, tuple(held)),
        out_shape=jax.ShapeDtypeStruct((block, width), bf16),
        in_specs=[vmem] * 5 + [anywhere] * 4,
        out_specs=vmem,
        scratch_shapes=list(held.values()),
        compiler_params=pltpu.CompilerParams(
            collective_id=0, has_side_effects=True, vmem_limit_bytes=62 << 20
        ),
        name="layer",
    )(
        att,
        resid,
        gain,
        jnp.asarray(pick_local, bf16),
        jnp.asarray(pick_all, bf16),
        out_weight,
        gate_weight,
        up_weight,
        down_weight,
    )


def on_device(
    queries,
    cached_entries,
    new_entry,
    lengths,
    residual,
    out_weight,
    norm_gain,
    gate_weight,
    up_weight,
    down_weight,
):
    pools = lax.axis_size("pool")
    amount = queries.shape[0]
    attended = attend(queries, cached_entries, new_entry, lengths)
    att = attended.reshape(amount, pools, -1).transpose(1, 0, 2)
    att = jnp.pad(att, ((0, 0), (0, PAD - amount), (0, 0)))
    return finish_rows(
        att,
        residual,
        norm_gain.astype(jnp.float32)[None, :],
        out_weight,
        gate_weight,
        up_weight,
        down_weight,
        amount,
    )


def solution(mesh):
    placed = (
        P(("groups", "pool", "tp"), None),
        P(("groups", "pool", "tp"), None, None),
        P(("groups", "pool", "tp"), None),
        P(("groups", "pool", "tp")),
        P(("groups", "pool"), "tp"),
        P("pool", "tp"),
        P("tp"),
        P("tp", "pool"),
        P("tp", "pool"),
        P("pool", "tp"),
    )
    return jax.shard_map(
        on_device,
        mesh=mesh,
        in_specs=placed,
        out_specs=P(("groups", "pool"), "tp"),
        check_vma=False,
    )
```

```python
import functools
import math
import types

import jax
import jax.numpy as jnp
import numpy as np
from jax import lax
from jax.experimental import pallas as pl
from jax.experimental.pallas import tpu as pltpu
from jax.sharding import PartitionSpec as P

D = 7168
HEADS = 64
HD = 256


epsilon = 1e-06


PAD = 8
LAG = 3
BACK_LAG = 3
SLOTS = 8
CHUNKS = 4
MESH = pl.DeviceIdType.MESH


def tile_of(extent):
    return 256 if extent % 256 == 0 else 128


def sizes_of(pools, tps, amount, places, block, width, cols, ff):
    rows = block * pools
    wide = 256 if ff % 256 == 0 else 384
    parts = 2 if width % 256 == 0 else 1
    pieces = ff // wide
    group = 2 if pieces % 2 == 0 else 1
    return types.SimpleNamespace(
        pools=pools,
        tps=tps,
        chips=pools // 2,
        amount=amount,
        places=places,
        block=block,
        width=width,
        cols=cols,
        ff=ff,
        rows=rows,
        half=rows // 2,
        slab=pools * amount,
        chunk=cols // CHUNKS,
        parts=parts,
        part=width // parts,
        wide=wide,
        low=(wide // 256 * 128 if wide % 256 == 0 else 256, 128),
        pieces=pieces,
        group=group,
        groups=pieces // group,
        turn=max(pieces, pieces // group * (group - 1) + LAG * (tps - 1)),
        slots=min(SLOTS, pieces),
        lanes=-(-rows // 128) * 128,
        out_tile=width // parts if rows <= 256 else tile_of(width // parts),
    )


def scratch_of(z):
    bf16, f32 = jnp.bfloat16, jnp.float32
    dma = pltpu.SemaphoreType.DMA
    vmem = pltpu.VMEM
    held = {
        "cache": vmem((z.amount, z.places, 2 * HD), bf16),
        "flat": vmem((z.amount, z.pools * z.cols), bf16),
        "asked": vmem((z.amount, HEADS, HD), f32),
        "mixed": vmem((PAD, HEADS, HD), f32),
        "att": vmem((z.pools, PAD, z.cols), bf16),
        "cache_sem": dma((z.amount,)),
        "flat_sem": dma((1,)),
        "wo": vmem((z.cols, z.width), bf16),
        "wgu": vmem((z.slots, z.width, 2 * z.wide), bf16),
        "wd": vmem((z.ff, z.width), bf16),
        "raw": vmem((z.pools, PAD, z.cols), bf16),
        "slabs": vmem((z.tps, CHUNKS, z.slab, z.chunk), bf16),
        "x": vmem((z.rows, z.chunk), bf16),
        "pf": vmem((z.rows, z.width), f32),
        "pair_out": vmem((z.parts, z.half, z.part), bf16),
        "pair_in": vmem((z.parts, z.half, z.part), bf16),
        "chip_out": vmem((z.parts, z.half, z.part), bf16),
        "chip_in": vmem((z.chips, z.parts, z.half, z.part), bf16),
        "post": vmem((z.half, z.width), f32),
        "own_post": vmem((z.block, z.width), f32),
        "s_in": vmem((z.rows, z.width), bf16),
        "sq_half": vmem((8, z.lanes), f32),
        "sq_pair": vmem((8, z.lanes), f32),
        "sq_all": vmem((z.tps, 8, z.lanes), f32),
        "inv": vmem((z.rows, 128), f32),
        "sums": vmem((z.pieces, z.rows, 2 * z.wide), f32),
        "acc": vmem((z.rows, z.width), f32),
        "end_out": vmem((z.parts, z.half, z.part), bf16),
        "end_in": vmem((z.parts, z.half, z.part), bf16),
        "last_out": vmem((z.chips, z.parts, z.block, z.part), bf16),
        "last_in": vmem((z.chips, z.parts, z.block, z.part), bf16),
        "wo_sem": dma((CHUNKS,)),
        "wd_sem": dma((1,)),
        "g_sem": dma((z.slots,)),
        "u_sem": dma((z.slots,)),
        "a_send": dma((CHUNKS, z.pools)),
        "a_recv": dma((CHUNKS, z.pools)),
        "c_right": dma((z.tps, CHUNKS)),
        "c_left": dma((z.tps, CHUNKS)),
        "c_recv": dma((z.tps, CHUNKS)),
        "pair_send": dma((z.parts,)),
        "pair_recv": dma((z.parts,)),
        "chip_send": dma((z.chips, z.parts)),
        "chip_recv": dma((z.chips, z.parts)),
        "in_send": dma((z.parts,)),
        "in_recv": dma((z.parts,)),
        "sq_send": dma((1,)),
        "sq_recv": dma((1,)),
        "end_send": dma((z.parts,)),
        "end_recv": dma((z.parts,)),
        "last_send": dma((z.chips, z.parts)),
        "last_recv": dma((z.chips, z.parts)),
        "e_send": dma((2,)),
        "e_recv": dma((z.tps,)),
    }
    for s in range(2):
        held["sbuf%d" % s] = vmem((z.pieces, z.rows, 2 * z.low[s]), bf16)
        held["rbuf%d" % s] = vmem((z.pieces, z.rows, 2 * z.low[s]), bf16)
        held["hid%d" % s] = vmem((z.groups, z.group, z.rows, z.low[s]), bf16)
        for name in ("r_send", "r_recv"):
            held["%s%d" % (name, s)] = dma((z.pieces,))
        for name in ("h_send", "h_recv"):
            held["%s%d" % (name, s)] = dma((z.groups,))
    return held


def layer_kernel(
    z,
    names,
    lengths,
    fresh,
    resid,
    gain,
    pick_local,
    pick_all,
    queries_hbm,
    cache_hbm,
    wo_hbm,
    wg_hbm,
    wu_hbm,
    wd_hbm,
    out,
    *refs,
):
    v = types.SimpleNamespace(**dict(zip(names, refs)))
    att = v.att
    bf16, f32 = jnp.bfloat16, jnp.float32
    p = lax.axis_index("pool")
    t = lax.axis_index("tp")
    core, chip = lax.rem(p, 2), p // 2
    partner = p + 1 - 2 * core
    last = z.tps - 1
    before, behind = lax.rem(t + z.tps - 1, z.tps), lax.rem(t + 1, z.tps)
    mine = pl.ds(pl.multiple_of(core * z.half, 16), z.half)
    other = pl.ds(pl.multiple_of((1 - core) * z.half, 16), z.half)
    block_in_half = pl.ds(pl.multiple_of(chip * z.block, 8), z.block)
    low_at = (0, z.low[0])

    def span(j, extent):
        return pl.ds(pl.multiple_of(j * extent, 128), extent)

    def wo_copy(k):
        at = pl.ds(pl.multiple_of(k * z.chunk, 128), z.chunk)
        return pltpu.make_async_copy(wo_hbm.at[at], v.wo.at[at], v.wo_sem.at[k])

    def weight_copies(j):
        slot = lax.rem(j, z.slots)
        at = span(j, z.wide)
        return (
            pltpu.make_async_copy(wg_hbm.at[:, at], v.wgu.at[slot, :, pl.ds(0, z.wide)], v.g_sem.at[slot]),
            pltpu.make_async_copy(wu_hbm.at[:, at], v.wgu.at[slot, :, pl.ds(z.wide, z.wide)], v.u_sem.at[slot]),
        )

    wd_copy = pltpu.make_async_copy(wd_hbm, v.wd, v.wd_sem.at[0])

    def remote(src, dst, send, recv, device):
        return pltpu.make_async_remote_copy(
            src_ref=src, dst_ref=dst, send_sem=send, recv_sem=recv, device_id=device, device_id_type=MESH
        )

    def cache_copy(r):
        return pltpu.make_async_copy(cache_hbm.at[r], v.cache.at[r], v.cache_sem.at[r])

    flat_copy = pltpu.make_async_copy(queries_hbm, v.flat, v.flat_sem.at[0])
    flat_copy.start()
    for r in range(z.amount):
        cache_copy(r).start()
    for k in range(CHUNKS):
        wo_copy(k).start()

    barrier = pltpu.get_barrier_semaphore()
    for k in range(1, z.pools):
        pl.semaphore_signal(barrier, inc=1, device_id={"pool": lax.rem(p + k, z.pools)}, device_id_type=MESH)
    for k in range(1, z.tps):
        pl.semaphore_signal(barrier, inc=1, device_id={"tp": lax.rem(t + k, z.tps)}, device_id_type=MESH)

    def att_copy(j, k):
        q = lax.rem(p + j, z.pools)
        at = pl.ds(k * z.chunk, z.chunk)
        return remote(att.at[q, :, at], v.raw.at[p, :, at], v.a_send.at[k, j], v.a_recv.at[k, p], {"pool": q})

    def att_arrival(j, k):
        q = lax.rem(p + j, z.pools)
        at = pl.ds(k * z.chunk, z.chunk)
        return remote(att.at[q, :, at], v.raw.at[q, :, at], v.a_send.at[k, j], v.a_recv.at[k, q], {"pool": q})

    for j in range(z.slots):
        for copy in weight_copies(jnp.int32(j)):
            copy.start()
    wd_copy.start()

    flat_copy.wait()
    v.mixed[...] = jnp.zeros_like(v.mixed)
    for h in range(HEADS):
        v.asked[:, h, :] = v.flat[:, h * HD : (h + 1) * HD].astype(f32)

    def attend(r):
        factor = 1.0 / math.sqrt(HD)
        cache_copy(r).wait()
        heads = v.asked[r]
        new_row = fresh[r : r + 1, :].astype(f32)
        scores = (
            lax.dot_general(
                heads.astype(bf16), v.cache[r, :, :HD], (((1,), (1,)), ((), ())), preferred_element_type=f32
            )
            * factor
        )
        own_score = jnp.sum(heads * new_row[:, :HD], axis=1, keepdims=True) * factor
        positions = lax.broadcasted_iota(jnp.int32, scores.shape, 1)
        usable = positions < lengths[r]
        scores = jnp.where(usable, scores, -jnp.inf)
        peak_score = jnp.maximum(jnp.max(scores, axis=1, keepdims=True), own_score)
        weights_raw = jnp.where(usable, jnp.exp(scores - peak_score), 0.0)
        own_raw = jnp.exp(own_score - peak_score)
        share = 1.0 / (jnp.sum(weights_raw, axis=1, keepdims=True) + own_raw)
        weights = (weights_raw * share).astype(bf16)
        own_weight = (own_raw * share).astype(bf16).astype(f32)
        mixture = jnp.dot(weights, v.cache[r, :, HD:], preferred_element_type=f32)
        v.mixed[r] = mixture + own_weight * new_row[:, HD:]

    for r in range(z.amount):
        attend(r)
    pl.semaphore_wait(barrier, z.pools + z.tps - 2)
    per_chunk = z.chunk // HD
    for k in range(CHUNKS):
        for q in range(z.pools):
            for b in range(per_chunk):
                h = q * (z.cols // HD) + k * per_chunk + b
                at = pl.ds(k * z.chunk + b * HD, HD)
                v.att[q, :, at] = v.mixed[:, h, :].astype(bf16)
        for j in range(1, z.pools):
            att_copy(j, k).start()
    v.raw[p] = att[p]
    v.pf[...] = jnp.zeros_like(v.pf)

    def slab_right(origin, k):
        ref = v.slabs.at[origin, k]
        return remote(ref, ref, v.c_right.at[origin, k], v.c_recv.at[origin, k], {"tp": behind})

    def slab_left(origin, k):
        ref = v.slabs.at[origin, k]
        return remote(ref, ref, v.c_left.at[origin, k], v.c_recv.at[origin, k], {"tp": before})

    for k in range(CHUNKS):
        for j in range(1, z.pools):
            att_arrival(j, k).wait_recv()
        tall = jnp.concatenate([v.raw[q, :, pl.ds(k * z.chunk, z.chunk)].astype(f32) for q in range(z.pools)], axis=0)
        v.slabs[t, k] = jnp.dot(pick_local[...], tall.astype(bf16), preferred_element_type=f32).astype(bf16)

        @pl.when(t < last)
        def _():
            slab_right(t, k).start()

        @pl.when(t > 0)
        def _():
            slab_left(t, k).start()

    def gather_step(d, k):
        @pl.when(t - d >= 0)
        def _():
            slab_left(t - d, k).wait_recv()

            @pl.when(t < last)
            def _():
                slab_right(t - d, k).start()

        @pl.when(t + d <= last)
        def _():
            slab_right(t + d, k).wait_recv()

            @pl.when(t > 0)
            def _():
                slab_left(t + d, k).start()

    for d in range(1, last):
        pl.loop(0, CHUNKS)(functools.partial(gather_step, d))

    def rows_of(k):
        gather_step(last, k)
        tall = jnp.concatenate([v.slabs[o, k].astype(f32) for o in range(z.tps)], axis=0)
        v.x[...] = jnp.dot(pick_all[...], tall.astype(bf16), preferred_element_type=f32).astype(bf16)
        wo_copy(k).wait()

    def project(k, at):
        down_rows = pl.ds(pl.multiple_of(k * z.chunk, 128), z.chunk)
        v.pf[:, at] += jnp.dot(v.x[...], v.wo[down_rows, at], preferred_element_type=f32)

    @pl.loop(0, CHUNKS - 1)
    def _(k):
        rows_of(k)

        @pl.loop(0, z.width // z.out_tile)
        def _(n):
            project(k, span(n, z.out_tile))

    def pair_copy(n):
        return remote(
            v.pair_out.at[n], v.pair_in.at[n], v.pair_send.at[n], v.pair_recv.at[n], {"pool": partner}
        )

    def chip_copy(j, n):
        to = lax.rem(chip + j, z.chips)
        return remote(
            v.chip_out.at[n], v.chip_in.at[chip, n], v.chip_send.at[j, n], v.chip_recv.at[chip, n], {"pool": 2 * to + core}
        )

    def chip_arrival(j, n):
        to = lax.rem(chip + j, z.chips)
        return remote(
            v.chip_out.at[n], v.chip_in.at[to, n], v.chip_send.at[j, n], v.chip_recv.at[to, n], {"pool": 2 * to + core}
        )

    def in_copy(n):
        ref = v.s_in.at[mine, pl.ds(n * z.part, z.part)]
        return remote(ref, ref, v.in_send.at[n], v.in_recv.at[n], {"pool": partner})

    def in_arrival(n):
        ref = v.s_in.at[other, pl.ds(n * z.part, z.part)]
        return remote(ref, ref, v.in_send.at[n], v.in_recv.at[n], {"pool": partner})

    sq_copy = remote(v.sq_half, v.sq_pair, v.sq_send.at[0], v.sq_recv.at[0], {"pool": partner})

    rows_of(CHUNKS - 1)
    for n in range(z.parts):
        at = pl.ds(n * z.part, z.part)

        @pl.loop(0, z.part // z.out_tile)
        def _(m):
            project(CHUNKS - 1, pl.ds(pl.multiple_of(n * z.part + m * z.out_tile, 128), z.out_tile))

        v.pair_out[n] = v.pf[other, at].astype(bf16)
        pair_copy(n).start()

    for n in range(z.parts):
        at = pl.ds(n * z.part, z.part)
        pair_copy(n).wait_recv()
        v.post[:, at] = v.pf[mine, at] + v.pair_in[n].astype(f32)
        v.post[block_in_half, at] += resid[:, at].astype(f32)
        v.chip_out[n] = v.post[:, at].astype(bf16)
        for j in range(1, z.chips):
            chip_copy(j, n).start()

    squares = jnp.zeros((z.half, 1), f32)
    for n in range(z.parts):
        at = pl.ds(n * z.part, z.part)
        value = v.post[:, at]
        for j in range(1, z.chips):
            chip_arrival(j, n).wait_recv()
            value = value + v.chip_in[lax.rem(chip + j, z.chips), n].astype(f32)
        v.post[:, at] = value
        v.s_in[mine, at] = (value * gain[at].astype(f32)[None, :]).astype(bf16)
        in_copy(n).start()
        squares = squares + jnp.sum(value * value, axis=1, keepdims=True)

    lane = lax.broadcasted_iota(jnp.int32, (z.half, z.lanes), 1)
    row = lax.broadcasted_iota(jnp.int32, (z.half, z.lanes), 0) + core * z.half
    flat = jnp.sum(jnp.where(lane == row, squares, 0.0), axis=0, keepdims=True)
    v.sq_half[...] = jnp.broadcast_to(flat, (8, z.lanes))
    sq_copy.start()
    v.own_post[...] = v.post[block_in_half, :]
    v.acc[...] = jnp.zeros_like(v.acc)
    for n in range(z.parts):
        in_arrival(n).wait_recv()
    sq_copy.wait_recv()
    v.sq_all[t] = v.sq_half[...] + v.sq_pair[...]

    ends = (0, last)

    def square_copy(s):
        return remote(v.sq_all.at[t], v.sq_all.at[t], v.e_send.at[s], v.e_recv.at[t], {"tp": ends[s]})

    def square_arrival(o):
        return remote(v.sq_all.at[o], v.sq_all.at[o], v.e_send.at[0], v.e_recv.at[o], {"tp": o})

    for s in range(2):

        @pl.when(t != ends[s])
        def _():
            square_copy(s).start()

    def scale_rows():
        for o in range(z.tps):

            @pl.when(t != o)
            def _():
                square_arrival(o).wait_recv()

        total = v.sq_all[0]
        for o in range(1, z.tps):
            total = total + v.sq_all[o]
        lane = lax.broadcasted_iota(jnp.int32, (z.rows, z.lanes), 1)
        row = lax.broadcasted_iota(jnp.int32, (z.rows, z.lanes), 0)
        tall = jnp.sum(jnp.where(lane == row, total[0:1], 0.0), axis=1, keepdims=True)
        v.inv[...] = jnp.broadcast_to(lax.rsqrt(tall / D + epsilon), (z.rows, 128))

    hid = (v.hid0, v.hid1)
    sbuf, rbuf = (v.sbuf0, v.sbuf1), (v.rbuf0, v.rbuf1)
    r_send, r_recv = (v.r_send0, v.r_send1), (v.r_recv0, v.r_recv1)
    h_send, h_recv = (v.h_send0, v.h_send1), (v.h_recv0, v.h_recv1)

    def lanes(s):
        if s == 0:
            return last - t, before, behind
        return t, behind, before

    def sum_hop(s, j):
        return remote(sbuf[s].at[j], rbuf[s].at[j], r_send[s].at[j], r_recv[s].at[j], {"tp": lanes(s)[1]})

    def hidden_hop(s, j):
        return remote(hid[s].at[j], hid[s].at[j], h_send[s].at[j], h_recv[s].at[j], {"tp": lanes(s)[2]})

    def compute(j):
        for copy in weight_copies(j):
            copy.wait()
        v.sums[j] = jnp.dot(v.s_in[...], v.wgu[lax.rem(j, z.slots)], preferred_element_type=f32)

        @pl.when(j + z.slots < z.pieces)
        def _():
            for copy in weight_copies(j + z.slots):
                copy.start()

    def down(g, at):
        held = [hid[s][g, b] for b in range(z.group) for s in range(2)]
        extent = z.group * z.wide
        v.acc[:, at] += jnp.dot(
            jnp.concatenate(held, axis=1),
            v.wd[pl.ds(pl.multiple_of(g * extent, 128), extent), at],
            preferred_element_type=f32,
        )

    wd_copy.wait()
    compute(jnp.int32(0))
    def one_step(i):
        for s in range(2):
            far, _, _ = lanes(s)
            c = i - LAG * far
            at_gate = pl.ds(low_at[s], z.low[s])
            at_up = pl.ds(z.wide + low_at[s], z.low[s])

            def summed():
                gate = v.sums[c, :, at_gate] + rbuf[s][c, :, : z.low[s]].astype(f32)
                return gate, v.sums[c, :, at_up] + rbuf[s][c, :, z.low[s] :].astype(f32)

            def pass_on(gate, up):
                sbuf[s][c, :, : z.low[s]] = gate.astype(bf16)
                sbuf[s][c, :, z.low[s] :] = up.astype(bf16)
                sum_hop(s, c).start()

            inside = (c >= 0) & (c < z.pieces)

            @pl.when(inside & (far == 0))
            def _():
                pass_on(v.sums[c, :, at_gate], v.sums[c, :, at_up])

            @pl.when(inside & (far > 0) & (far < last))
            def _():
                sum_hop(s, c).wait_recv()
                pass_on(*summed())

            @pl.when(inside & (far == last))
            def _():
                @pl.when(c == 0)
                def _():
                    scale_rows()

                sum_hop(s, c).wait_recv()
                inv = v.inv[:, :1]
                gate, up = summed()
                gate, up = gate * inv, up * inv
                hid[s][lax.div(c, z.group), lax.rem(c, z.group)] = (gate / (1.0 + jnp.exp(-gate)) * up).astype(bf16)

        for s in range(2):
            far, _, _ = lanes(s)
            back = last - far
            g = i - z.turn - BACK_LAG * back

            @pl.when((g >= 0) & (g < z.groups))
            def _():
                @pl.when(back > 0)
                def _():
                    hidden_hop(s, g).wait_recv()

                @pl.when(back < last)
                def _():
                    hidden_hop(s, g).start()

        @pl.when(i + 1 < z.pieces)
        def _():
            compute(i + 1)

        g = i - z.turn - BACK_LAG * jnp.maximum(t, last - t)

        @pl.when((g >= 0) & (g < z.groups - 1))
        def _():
            @pl.loop(0, z.width // z.out_tile)
            def _(n):
                down(g, span(n, z.out_tile))

    pl.loop(0, z.turn + z.groups + BACK_LAG * last)(one_step)

    def end_copy(n):
        return remote(v.end_out.at[n], v.end_in.at[n], v.end_send.at[n], v.end_recv.at[n], {"pool": partner})

    def last_copy(j, n):
        to = lax.rem(chip + j, z.chips)
        return remote(
            v.last_out.at[to, n], v.last_in.at[chip, n], v.last_send.at[j, n], v.last_recv.at[chip, n], {"pool": 2 * to + core}
        )

    def last_arrival(j, n):
        to = lax.rem(chip + j, z.chips)
        return remote(
            v.last_out.at[to, n], v.last_in.at[to, n], v.last_send.at[j, n], v.last_recv.at[to, n], {"pool": 2 * to + core}
        )

    for n in range(z.parts):

        @pl.loop(0, z.part // z.out_tile)
        def _(m):
            down(z.groups - 1, pl.ds(pl.multiple_of(n * z.part + m * z.out_tile, 128), z.out_tile))

        v.end_out[n] = v.acc[other, pl.ds(n * z.part, z.part)].astype(bf16)
        end_copy(n).start()
    for n in range(z.parts):
        at = pl.ds(n * z.part, z.part)
        end_copy(n).wait_recv()
        v.post[:, at] = v.acc[mine, at] + v.end_in[n].astype(f32)
        for q in range(z.chips):
            v.last_out[q, n] = v.post[pl.ds(q * z.block, z.block), at].astype(bf16)
        for j in range(1, z.chips):
            last_copy(j, n).start()
    for n in range(z.parts):
        at = pl.ds(n * z.part, z.part)
        total = v.own_post[:, at] + v.post[block_in_half, at]
        for j in range(1, z.chips):
            last_arrival(j, n).wait_recv()
            total = total + v.last_in[lax.rem(chip + j, z.chips), n].astype(f32)
        out[:, at] = total.astype(bf16)

    for j in range(1, z.pools):
        for k in range(CHUNKS):
            att_copy(j, k).wait_send()
    for n in range(z.parts):
        pair_copy(n).wait_send()
        in_copy(n).wait_send()
        end_copy(n).wait_send()
        for j in range(1, z.chips):
            chip_copy(j, n).wait_send()
            last_copy(j, n).wait_send()
    sq_copy.wait_send()
    for s in range(2):

        @pl.when(t != ends[s])
        def _():
            square_copy(s).wait_send()

    @pl.loop(0, CHUNKS)
    def _(k):
        for origin in range(z.tps):

            @pl.when((t < last) & (origin <= t))
            def _():
                slab_right(origin, k).wait_send()

            @pl.when((t > 0) & (origin >= t))
            def _():
                slab_left(origin, k).wait_send()

    @pl.loop(0, z.pieces)
    def _(c):
        for s in range(2):
            far, _, _ = lanes(s)

            @pl.when(far < last)
            def _():
                sum_hop(s, c).wait_send()

            @pl.when((far > 0) & (c < z.groups))
            def _():
                hidden_hop(s, c).wait_send()


def on_device(
    queries,
    cached_entries,
    new_entry,
    lengths,
    residual,
    out_weight,
    norm_gain,
    gate_weight,
    up_weight,
    down_weight,
):
    pools, tps = lax.axis_size("pool"), lax.axis_size("tp")
    amount, cols = queries.shape[0], queries.shape[1] // pools
    block, width = residual.shape
    z = sizes_of(pools, tps, amount, cached_entries.shape[1], block, width, cols, gate_weight.shape[1])

    local = np.arange(z.slab)
    pick_local = np.zeros((z.slab, pools * PAD), np.float32)
    pick_local[local, local // amount * PAD + local % amount] = 1
    every = np.arange(z.rows)
    of_core, of_chip = every // z.half, every % z.half // block
    of_tp, of_row = every // amount % tps, every % amount
    pick_all = np.zeros((z.rows, z.rows), np.float32)
    pick_all[every, (of_tp * pools + 2 * of_chip + of_core) * amount + of_row] = 1

    vmem = pl.BlockSpec(memory_space=pltpu.VMEM)
    anywhere = pl.BlockSpec(memory_space=pl.ANY)
    bf16 = jnp.bfloat16
    held = scratch_of(z)
    return pl.pallas_call(
        functools.partial(layer_kernel, z, tuple(held)),
        out_shape=jax.ShapeDtypeStruct((block, width), bf16),
        in_specs=[pl.BlockSpec(memory_space=pltpu.SMEM)] + [vmem] * 5 + [anywhere] * 6,
        out_specs=vmem,
        scratch_shapes=list(held.values()),
        compiler_params=pltpu.CompilerParams(
            collective_id=0, has_side_effects=True, vmem_limit_bytes=62 << 20
        ),
        name="layer",
    )(
        lengths,
        new_entry,
        residual,
        norm_gain,
        jnp.asarray(pick_local, bf16),
        jnp.asarray(pick_all, bf16),
        queries,
        cached_entries,
        out_weight,
        gate_weight,
        up_weight,
        down_weight,
    )


def solution(mesh):
    placed = (
        P(("groups", "pool", "tp"), None),
        P(("groups", "pool", "tp"), None, None),
        P(("groups", "pool", "tp"), None),
        P(("groups", "pool", "tp")),
        P(("groups", "pool"), "tp"),
        P("pool", "tp"),
        P("tp"),
        P("tp", "pool"),
        P("tp", "pool"),
        P("pool", "tp"),
    )
    return jax.shard_map(
        on_device,
        mesh=mesh,
        in_specs=placed,
        out_specs=P(("groups", "pool"), "tp"),
        check_vma=False,
    )
```

```python
import functools
import math
import types

import jax
import jax.numpy as jnp
import numpy as np
from jax import lax
from jax.experimental import pallas as pl
from jax.experimental.pallas import tpu as pltpu
from jax.sharding import PartitionSpec as P

D = 7168
HEADS = 64
HD = 256


epsilon = 1e-06


PAD = 8
LAG = 3
BACK_LAG = 3
SLOTS = 8
CHUNKS = 4
MESH = pl.DeviceIdType.MESH


def tile_of(extent):
    return 256 if extent % 256 == 0 else 128


def sizes_of(pools, tps, amount, places, block, width, cols, ff):
    rows = block * pools
    wide = 256 if ff % 256 == 0 else 384
    parts = 2 if width % 256 == 0 else 1
    pieces = ff // wide
    group = 2 if pieces % 2 == 0 else 1
    return types.SimpleNamespace(
        pools=pools,
        tps=tps,
        chips=pools // 2,
        amount=amount,
        places=places,
        block=block,
        width=width,
        cols=cols,
        ff=ff,
        rows=rows,
        half=rows // 2,
        slab=pools * amount,
        chunk=cols // CHUNKS,
        parts=parts,
        part=width // parts,
        wide=wide,
        low=(wide // 256 * 128 if wide % 256 == 0 else 256, 128),
        pieces=pieces,
        group=group,
        groups=pieces // group,
        turn=max(pieces, pieces // group * (group - 1) + LAG * (tps - 1)),
        slots=min(SLOTS, pieces),
        lanes=-(-rows // 128) * 128,
        out_tile=width // parts if rows <= 256 else tile_of(width // parts),
    )


def scratch_of(z):
    bf16, f32 = jnp.bfloat16, jnp.float32
    dma = pltpu.SemaphoreType.DMA
    vmem = pltpu.VMEM
    held = {
        "cache": vmem((z.amount, z.places, 2 * HD), bf16),
        "flat": vmem((z.amount, z.pools * z.cols), bf16),
        "asked": vmem((2, z.amount, HEADS // 2, HD), f32),
        "mixed": vmem((2, PAD, HEADS // 2, HD), f32),
        "resid": vmem((z.block, z.width), bf16),
        "gain": vmem((z.width,), bf16),
        "pick_local": vmem((z.slab, z.pools * PAD), bf16),
        "pick_all": vmem((z.rows, z.rows), bf16),
        "small_sem": dma((4,)),
        "att": vmem((z.pools, PAD, z.cols), bf16),
        "cache_sem": dma((z.amount,)),
        "flat_sem": dma((1,)),
        "wo": vmem((z.cols, z.width), bf16),
        "wgu": vmem((z.slots, z.width, 2 * z.wide), bf16),
        "wd": vmem((z.ff, z.width), bf16),
        "raw": vmem((z.pools, PAD, z.cols), bf16),
        "slabs": vmem((z.tps, CHUNKS, z.slab, z.chunk), bf16),
        "x": vmem((z.rows, z.chunk), bf16),
        "pf": vmem((z.rows, z.width), f32),
        "pair_out": vmem((z.parts, z.half, z.part), bf16),
        "pair_in": vmem((z.parts, z.half, z.part), bf16),
        "chip_out": vmem((z.parts, z.half, z.part), bf16),
        "chip_in": vmem((z.chips, z.parts, z.half, z.part), bf16),
        "post": vmem((z.half, z.width), f32),
        "own_post": vmem((z.block, z.width), f32),
        "s_in": vmem((z.rows, z.width), bf16),
        "sq_half": vmem((8, z.lanes), f32),
        "sq_pair": vmem((8, z.lanes), f32),
        "sq_all": vmem((z.tps, 8, z.lanes), f32),
        "inv": vmem((z.rows, 128), f32),
        "sums": vmem((z.pieces, z.rows, 2 * z.wide), f32),
        "acc": vmem((z.rows, z.width), f32),
        "end_out": vmem((z.parts, z.half, z.part), bf16),
        "end_in": vmem((z.parts, z.half, z.part), bf16),
        "last_out": vmem((z.chips, z.parts, z.block, z.part), bf16),
        "last_in": vmem((z.chips, z.parts, z.block, z.part), bf16),
        "wo_sem": dma((CHUNKS,)),
        "wd_sem": dma((1,)),
        "g_sem": dma((z.slots,)),
        "u_sem": dma((z.slots,)),
        "a_send": dma((CHUNKS, z.pools)),
        "a_recv": dma((CHUNKS, z.pools)),
        "c_right": dma((z.tps, CHUNKS)),
        "c_left": dma((z.tps, CHUNKS)),
        "c_recv": dma((z.tps, CHUNKS)),
        "pair_send": dma((z.parts,)),
        "pair_recv": dma((z.parts,)),
        "chip_send": dma((z.chips, z.parts)),
        "chip_recv": dma((z.chips, z.parts)),
        "in_send": dma((z.parts,)),
        "in_recv": dma((z.parts,)),
        "sq_send": dma((1,)),
        "sq_recv": dma((1,)),
        "end_send": dma((z.parts,)),
        "end_recv": dma((z.parts,)),
        "last_send": dma((z.chips, z.parts)),
        "last_recv": dma((z.chips, z.parts)),
        "e_send": dma((2,)),
        "e_recv": dma((z.tps,)),
    }
    for s in range(2):
        held["sbuf%d" % s] = vmem((z.pieces, z.rows, 2 * z.low[s]), bf16)
        held["rbuf%d" % s] = vmem((z.pieces, z.rows, 2 * z.low[s]), bf16)
        held["hid%d" % s] = vmem((z.groups, z.group, z.rows, z.low[s]), bf16)
        for name in ("r_send", "r_recv"):
            held["%s%d" % (name, s)] = dma((z.pieces,))
        for name in ("h_send", "h_recv"):
            held["%s%d" % (name, s)] = dma((z.groups,))
    return held


def layer_kernel(
    z,
    names,
    lengths,
    fresh,
    queries_hbm,
    resid_hbm,
    gain_hbm,
    pick_local_hbm,
    pick_all_hbm,
    cache_hbm,
    wo_hbm,
    wg_hbm,
    wu_hbm,
    wd_hbm,
    out,
    *refs,
):
    v = types.SimpleNamespace(**dict(zip(names, refs)))
    att, resid, gain, pick_local, pick_all = v.att, v.resid, v.gain, v.pick_local, v.pick_all
    bf16, f32 = jnp.bfloat16, jnp.float32
    p = lax.axis_index("pool")
    t = lax.axis_index("tp")
    core, chip = lax.rem(p, 2), p // 2
    partner = p + 1 - 2 * core
    last = z.tps - 1
    before, behind = lax.rem(t + z.tps - 1, z.tps), lax.rem(t + 1, z.tps)
    mine = pl.ds(pl.multiple_of(core * z.half, 16), z.half)
    other = pl.ds(pl.multiple_of((1 - core) * z.half, 16), z.half)
    block_in_half = pl.ds(pl.multiple_of(chip * z.block, 8), z.block)
    low_at = (0, z.low[0])

    def span(j, extent):
        return pl.ds(pl.multiple_of(j * extent, 128), extent)

    def wo_copy(k):
        at = pl.ds(pl.multiple_of(k * z.chunk, 128), z.chunk)
        return pltpu.make_async_copy(wo_hbm.at[at], v.wo.at[at], v.wo_sem.at[k])

    def weight_copies(j):
        slot = lax.rem(j, z.slots)
        at = span(j, z.wide)
        return (
            pltpu.make_async_copy(wg_hbm.at[:, at], v.wgu.at[slot, :, pl.ds(0, z.wide)], v.g_sem.at[slot]),
            pltpu.make_async_copy(wu_hbm.at[:, at], v.wgu.at[slot, :, pl.ds(z.wide, z.wide)], v.u_sem.at[slot]),
        )

    wd_copy = pltpu.make_async_copy(wd_hbm, v.wd, v.wd_sem.at[0])

    def remote(src, dst, send, recv, device):
        return pltpu.make_async_remote_copy(
            src_ref=src, dst_ref=dst, send_sem=send, recv_sem=recv, device_id=device, device_id_type=MESH
        )

    def cache_copy(r):
        return pltpu.make_async_copy(cache_hbm.at[r], v.cache.at[r], v.cache_sem.at[r])

    flat_copy = pltpu.make_async_copy(queries_hbm, v.flat, v.flat_sem.at[0])
    flat_copy.start()
    for r in range(z.amount):
        cache_copy(r).start()
    small_copies = [
        pltpu.make_async_copy(src, dst, v.small_sem.at[i])
        for i, (src, dst) in enumerate(
            ((resid_hbm, resid), (gain_hbm, gain), (pick_local_hbm, pick_local), (pick_all_hbm, pick_all))
        )
    ]
    for copy in small_copies:
        copy.start()

    barrier = pltpu.get_barrier_semaphore()
    for k in range(1, z.pools):
        pl.semaphore_signal(barrier, inc=1, device_id={"pool": lax.rem(p + k, z.pools)}, device_id_type=MESH)
    for k in range(1, z.tps):
        pl.semaphore_signal(barrier, inc=1, device_id={"tp": lax.rem(t + k, z.tps)}, device_id_type=MESH)

    def att_copy(j, k):
        q = lax.rem(p + j, z.pools)
        at = pl.ds(k * z.chunk, z.chunk)
        return remote(att.at[q, :, at], v.raw.at[p, :, at], v.a_send.at[k, j], v.a_recv.at[k, p], {"pool": q})

    def att_arrival(j, k):
        q = lax.rem(p + j, z.pools)
        at = pl.ds(k * z.chunk, z.chunk)
        return remote(att.at[q, :, at], v.raw.at[q, :, at], v.a_send.at[k, j], v.a_recv.at[k, q], {"pool": q})


    flat_copy.wait()
    v.mixed[...] = jnp.zeros_like(v.mixed)
    per_block = HEADS // z.pools
    held_heads = per_block // 2

    def attend(part, r):
        factor = 1.0 / math.sqrt(HD)
        heads = v.asked[part, r]
        new_row = fresh[r : r + 1, :].astype(f32)
        scores = (
            lax.dot_general(
                heads.astype(bf16), v.cache[r, :, :HD], (((1,), (1,)), ((), ())), preferred_element_type=f32
            )
            * factor
        )
        own_score = jnp.sum(heads * new_row[:, :HD], axis=1, keepdims=True) * factor
        positions = lax.broadcasted_iota(jnp.int32, scores.shape, 1)
        usable = positions < lengths[r]
        scores = jnp.where(usable, scores, -jnp.inf)
        peak_score = jnp.maximum(jnp.max(scores, axis=1, keepdims=True), own_score)
        weights_raw = jnp.where(usable, jnp.exp(scores - peak_score), 0.0)
        own_raw = jnp.exp(own_score - peak_score)
        share = 1.0 / (jnp.sum(weights_raw, axis=1, keepdims=True) + own_raw)
        weights = (weights_raw * share).astype(bf16)
        own_weight = (own_raw * share).astype(bf16).astype(f32)
        mixture = jnp.dot(weights, v.cache[r, :, HD:], preferred_element_type=f32)
        v.mixed[part, r] = mixture + own_weight * new_row[:, HD:]

    for r in range(z.amount):
        cache_copy(r).wait()
    for part in range(2):
        for q in range(z.pools):
            for b in range(held_heads):
                at = (q * per_block + part * held_heads + b) * HD
                v.asked[part, :, q * held_heads + b, :] = v.flat[:, at : at + HD].astype(f32)
        for r in range(z.amount):
            attend(part, r)
        for q in range(z.pools):
            for b in range(held_heads):
                at = pl.ds((part * held_heads + b) * HD, HD)
                v.att[q, :, at] = v.mixed[part, :, q * held_heads + b, :].astype(bf16)
        if part == 0:
            pl.semaphore_wait(barrier, z.pools + z.tps - 2)
        for k in range(part * CHUNKS // 2, (part + 1) * CHUNKS // 2):
            for j in range(1, z.pools):
                att_copy(j, k).start()
    for k in range(CHUNKS):
        wo_copy(k).start()
    for copy in small_copies:
        copy.wait()
    v.raw[p] = att[p]
    v.pf[...] = jnp.zeros_like(v.pf)

    def slab_right(origin, k):
        ref = v.slabs.at[origin, k]
        return remote(ref, ref, v.c_right.at[origin, k], v.c_recv.at[origin, k], {"tp": behind})

    def slab_left(origin, k):
        ref = v.slabs.at[origin, k]
        return remote(ref, ref, v.c_left.at[origin, k], v.c_recv.at[origin, k], {"tp": before})

    for k in range(CHUNKS):
        for j in range(1, z.pools):
            att_arrival(j, k).wait_recv()
        tall = jnp.concatenate([v.raw[q, :, pl.ds(k * z.chunk, z.chunk)].astype(f32) for q in range(z.pools)], axis=0)
        v.slabs[t, k] = jnp.dot(pick_local[...], tall.astype(bf16), preferred_element_type=f32).astype(bf16)

        @pl.when(t < last)
        def _():
            slab_right(t, k).start()

        @pl.when(t > 0)
        def _():
            slab_left(t, k).start()

    for j in range(z.slots):
        for copy in weight_copies(jnp.int32(j)):
            copy.start()
    wd_copy.start()
    def gather_step(d, k):
        @pl.when(t - d >= 0)
        def _():
            slab_left(t - d, k).wait_recv()

            @pl.when(t < last)
            def _():
                slab_right(t - d, k).start()

        @pl.when(t + d <= last)
        def _():
            slab_right(t + d, k).wait_recv()

            @pl.when(t > 0)
            def _():
                slab_left(t + d, k).start()

    for d in range(1, last):
        pl.loop(0, CHUNKS)(functools.partial(gather_step, d))

    def rows_of(k):
        gather_step(last, k)
        tall = jnp.concatenate([v.slabs[o, k].astype(f32) for o in range(z.tps)], axis=0)
        v.x[...] = jnp.dot(pick_all[...], tall.astype(bf16), preferred_element_type=f32).astype(bf16)
        wo_copy(k).wait()

    def project(k, at):
        down_rows = pl.ds(pl.multiple_of(k * z.chunk, 128), z.chunk)
        v.pf[:, at] += jnp.dot(v.x[...], v.wo[down_rows, at], preferred_element_type=f32)

    @pl.loop(0, CHUNKS - 1)
    def _(k):
        rows_of(k)

        @pl.loop(0, z.width // z.out_tile)
        def _(n):
            project(k, span(n, z.out_tile))

    def pair_copy(n):
        return remote(
            v.pair_out.at[n], v.pair_in.at[n], v.pair_send.at[n], v.pair_recv.at[n], {"pool": partner}
        )

    def chip_copy(j, n):
        to = lax.rem(chip + j, z.chips)
        return remote(
            v.chip_out.at[n], v.chip_in.at[chip, n], v.chip_send.at[j, n], v.chip_recv.at[chip, n], {"pool": 2 * to + core}
        )

    def chip_arrival(j, n):
        to = lax.rem(chip + j, z.chips)
        return remote(
            v.chip_out.at[n], v.chip_in.at[to, n], v.chip_send.at[j, n], v.chip_recv.at[to, n], {"pool": 2 * to + core}
        )

    def in_copy(n):
        ref = v.s_in.at[mine, pl.ds(n * z.part, z.part)]
        return remote(ref, ref, v.in_send.at[n], v.in_recv.at[n], {"pool": partner})

    def in_arrival(n):
        ref = v.s_in.at[other, pl.ds(n * z.part, z.part)]
        return remote(ref, ref, v.in_send.at[n], v.in_recv.at[n], {"pool": partner})

    sq_copy = remote(v.sq_half, v.sq_pair, v.sq_send.at[0], v.sq_recv.at[0], {"pool": partner})

    rows_of(CHUNKS - 1)
    for n in range(z.parts):
        at = pl.ds(n * z.part, z.part)

        @pl.loop(0, z.part // z.out_tile)
        def _(m):
            project(CHUNKS - 1, pl.ds(pl.multiple_of(n * z.part + m * z.out_tile, 128), z.out_tile))

        v.pair_out[n] = v.pf[other, at].astype(bf16)
        pair_copy(n).start()

    for n in range(z.parts):
        at = pl.ds(n * z.part, z.part)
        pair_copy(n).wait_recv()
        v.post[:, at] = v.pf[mine, at] + v.pair_in[n].astype(f32)
        v.post[block_in_half, at] += resid[:, at].astype(f32)
        v.chip_out[n] = v.post[:, at].astype(bf16)
        for j in range(1, z.chips):
            chip_copy(j, n).start()

    squares = jnp.zeros((z.half, 1), f32)
    for n in range(z.parts):
        at = pl.ds(n * z.part, z.part)
        value = v.post[:, at]
        for j in range(1, z.chips):
            chip_arrival(j, n).wait_recv()
            value = value + v.chip_in[lax.rem(chip + j, z.chips), n].astype(f32)
        v.post[:, at] = value
        v.s_in[mine, at] = (value * gain[at].astype(f32)[None, :]).astype(bf16)
        in_copy(n).start()
        squares = squares + jnp.sum(value * value, axis=1, keepdims=True)

    lane = lax.broadcasted_iota(jnp.int32, (z.half, z.lanes), 1)
    row = lax.broadcasted_iota(jnp.int32, (z.half, z.lanes), 0) + core * z.half
    flat = jnp.sum(jnp.where(lane == row, squares, 0.0), axis=0, keepdims=True)
    v.sq_half[...] = jnp.broadcast_to(flat, (8, z.lanes))
    sq_copy.start()
    v.own_post[...] = v.post[block_in_half, :]
    v.acc[...] = jnp.zeros_like(v.acc)
    for n in range(z.parts):
        in_arrival(n).wait_recv()
    sq_copy.wait_recv()
    v.sq_all[t] = v.sq_half[...] + v.sq_pair[...]

    ends = (0, last)

    def square_copy(s):
        return remote(v.sq_all.at[t], v.sq_all.at[t], v.e_send.at[s], v.e_recv.at[t], {"tp": ends[s]})

    def square_arrival(o):
        return remote(v.sq_all.at[o], v.sq_all.at[o], v.e_send.at[0], v.e_recv.at[o], {"tp": o})

    for s in range(2):

        @pl.when(t != ends[s])
        def _():
            square_copy(s).start()

    def scale_rows():
        for o in range(z.tps):

            @pl.when(t != o)
            def _():
                square_arrival(o).wait_recv()

        total = v.sq_all[0]
        for o in range(1, z.tps):
            total = total + v.sq_all[o]
        lane = lax.broadcasted_iota(jnp.int32, (z.rows, z.lanes), 1)
        row = lax.broadcasted_iota(jnp.int32, (z.rows, z.lanes), 0)
        tall = jnp.sum(jnp.where(lane == row, total[0:1], 0.0), axis=1, keepdims=True)
        v.inv[...] = jnp.broadcast_to(lax.rsqrt(tall / D + epsilon), (z.rows, 128))

    hid = (v.hid0, v.hid1)
    sbuf, rbuf = (v.sbuf0, v.sbuf1), (v.rbuf0, v.rbuf1)
    r_send, r_recv = (v.r_send0, v.r_send1), (v.r_recv0, v.r_recv1)
    h_send, h_recv = (v.h_send0, v.h_send1), (v.h_recv0, v.h_recv1)

    def lanes(s):
        if s == 0:
            return last - t, before, behind
        return t, behind, before

    def sum_hop(s, j):
        return remote(sbuf[s].at[j], rbuf[s].at[j], r_send[s].at[j], r_recv[s].at[j], {"tp": lanes(s)[1]})

    def hidden_hop(s, j):
        return remote(hid[s].at[j], hid[s].at[j], h_send[s].at[j], h_recv[s].at[j], {"tp": lanes(s)[2]})

    def compute(j):
        for copy in weight_copies(j):
            copy.wait()
        v.sums[j] = jnp.dot(v.s_in[...], v.wgu[lax.rem(j, z.slots)], preferred_element_type=f32)

        @pl.when(j + z.slots < z.pieces)
        def _():
            for copy in weight_copies(j + z.slots):
                copy.start()

    def down(g, at):
        held = [hid[s][g, b] for b in range(z.group) for s in range(2)]
        extent = z.group * z.wide
        v.acc[:, at] += jnp.dot(
            jnp.concatenate(held, axis=1),
            v.wd[pl.ds(pl.multiple_of(g * extent, 128), extent), at],
            preferred_element_type=f32,
        )

    wd_copy.wait()
    compute(jnp.int32(0))
    def one_step(i):
        for s in range(2):
            far, _, _ = lanes(s)
            c = i - LAG * far
            at_gate = pl.ds(low_at[s], z.low[s])
            at_up = pl.ds(z.wide + low_at[s], z.low[s])

            def summed():
                gate = v.sums[c, :, at_gate] + rbuf[s][c, :, : z.low[s]].astype(f32)
                return gate, v.sums[c, :, at_up] + rbuf[s][c, :, z.low[s] :].astype(f32)

            def pass_on(gate, up):
                sbuf[s][c, :, : z.low[s]] = gate.astype(bf16)
                sbuf[s][c, :, z.low[s] :] = up.astype(bf16)
                sum_hop(s, c).start()

            inside = (c >= 0) & (c < z.pieces)

            @pl.when(inside & (far == 0))
            def _():
                pass_on(v.sums[c, :, at_gate], v.sums[c, :, at_up])

            @pl.when(inside & (far > 0) & (far < last))
            def _():
                sum_hop(s, c).wait_recv()
                pass_on(*summed())

            @pl.when(inside & (far == last))
            def _():
                @pl.when(c == 0)
                def _():
                    scale_rows()

                sum_hop(s, c).wait_recv()
                inv = v.inv[:, :1]
                gate, up = summed()
                gate, up = gate * inv, up * inv
                hid[s][lax.div(c, z.group), lax.rem(c, z.group)] = (gate / (1.0 + jnp.exp(-gate)) * up).astype(bf16)

        for s in range(2):
            far, _, _ = lanes(s)
            back = last - far
            g = i - z.turn - BACK_LAG * back

            @pl.when((g >= 0) & (g < z.groups))
            def _():
                @pl.when(back > 0)
                def _():
                    hidden_hop(s, g).wait_recv()

                @pl.when(back < last)
                def _():
                    hidden_hop(s, g).start()

        @pl.when(i + 1 < z.pieces)
        def _():
            compute(i + 1)

        g = i - z.turn - BACK_LAG * jnp.maximum(t, last - t)

        @pl.when((g >= 0) & (g < z.groups - 1))
        def _():
            @pl.loop(0, z.width // z.out_tile)
            def _(n):
                down(g, span(n, z.out_tile))

    pl.loop(0, z.turn + z.groups + BACK_LAG * last)(one_step)

    def end_copy(n):
        return remote(v.end_out.at[n], v.end_in.at[n], v.end_send.at[n], v.end_recv.at[n], {"pool": partner})

    def last_copy(j, n):
        to = lax.rem(chip + j, z.chips)
        return remote(
            v.last_out.at[to, n], v.last_in.at[chip, n], v.last_send.at[j, n], v.last_recv.at[chip, n], {"pool": 2 * to + core}
        )

    def last_arrival(j, n):
        to = lax.rem(chip + j, z.chips)
        return remote(
            v.last_out.at[to, n], v.last_in.at[to, n], v.last_send.at[j, n], v.last_recv.at[to, n], {"pool": 2 * to + core}
        )

    for n in range(z.parts):

        @pl.loop(0, z.part // z.out_tile)
        def _(m):
            down(z.groups - 1, pl.ds(pl.multiple_of(n * z.part + m * z.out_tile, 128), z.out_tile))

        v.end_out[n] = v.acc[other, pl.ds(n * z.part, z.part)].astype(bf16)
        end_copy(n).start()
    for n in range(z.parts):
        at = pl.ds(n * z.part, z.part)
        end_copy(n).wait_recv()
        v.post[:, at] = v.acc[mine, at] + v.end_in[n].astype(f32)
        for q in range(z.chips):
            v.last_out[q, n] = v.post[pl.ds(q * z.block, z.block), at].astype(bf16)
        for j in range(1, z.chips):
            last_copy(j, n).start()
    for n in range(z.parts):
        at = pl.ds(n * z.part, z.part)
        total = v.own_post[:, at] + v.post[block_in_half, at]
        for j in range(1, z.chips):
            last_arrival(j, n).wait_recv()
            total = total + v.last_in[lax.rem(chip + j, z.chips), n].astype(f32)
        out[:, at] = total.astype(bf16)

    for j in range(1, z.pools):
        for k in range(CHUNKS):
            att_copy(j, k).wait_send()
    for n in range(z.parts):
        pair_copy(n).wait_send()
        in_copy(n).wait_send()
        end_copy(n).wait_send()
        for j in range(1, z.chips):
            chip_copy(j, n).wait_send()
            last_copy(j, n).wait_send()
    sq_copy.wait_send()
    for s in range(2):

        @pl.when(t != ends[s])
        def _():
            square_copy(s).wait_send()

    @pl.loop(0, CHUNKS)
    def _(k):
        for origin in range(z.tps):

            @pl.when((t < last) & (origin <= t))
            def _():
                slab_right(origin, k).wait_send()

            @pl.when((t > 0) & (origin >= t))
            def _():
                slab_left(origin, k).wait_send()

    @pl.loop(0, z.pieces)
    def _(c):
        for s in range(2):
            far, _, _ = lanes(s)

            @pl.when(far < last)
            def _():
                sum_hop(s, c).wait_send()

            @pl.when((far > 0) & (c < z.groups))
            def _():
                hidden_hop(s, c).wait_send()


def on_device(
    queries,
    cached_entries,
    new_entry,
    lengths,
    residual,
    out_weight,
    norm_gain,
    gate_weight,
    up_weight,
    down_weight,
):
    pools, tps = lax.axis_size("pool"), lax.axis_size("tp")
    amount, cols = queries.shape[0], queries.shape[1] // pools
    block, width = residual.shape
    z = sizes_of(pools, tps, amount, cached_entries.shape[1], block, width, cols, gate_weight.shape[1])

    local = np.arange(z.slab)
    pick_local = np.zeros((z.slab, pools * PAD), np.float32)
    pick_local[local, local // amount * PAD + local % amount] = 1
    every = np.arange(z.rows)
    of_core, of_chip = every // z.half, every % z.half // block
    of_tp, of_row = every // amount % tps, every % amount
    pick_all = np.zeros((z.rows, z.rows), np.float32)
    pick_all[every, (of_tp * pools + 2 * of_chip + of_core) * amount + of_row] = 1

    vmem = pl.BlockSpec(memory_space=pltpu.VMEM)
    anywhere = pl.BlockSpec(memory_space=pl.ANY)
    bf16 = jnp.bfloat16
    held = scratch_of(z)
    return pl.pallas_call(
        functools.partial(layer_kernel, z, tuple(held)),
        out_shape=jax.ShapeDtypeStruct((block, width), bf16),
        in_specs=[pl.BlockSpec(memory_space=pltpu.SMEM), vmem] + [anywhere] * 10,
        out_specs=vmem,
        scratch_shapes=list(held.values()),
        compiler_params=pltpu.CompilerParams(
            collective_id=0, has_side_effects=True, vmem_limit_bytes=62 << 20
        ),
        name="layer",
    )(
        lengths,
        new_entry,
        queries,
        residual,
        norm_gain,
        jnp.asarray(pick_local, bf16),
        jnp.asarray(pick_all, bf16),
        cached_entries,
        out_weight,
        gate_weight,
        up_weight,
        down_weight,
    )


def solution(mesh):
    placed = (
        P(("groups", "pool", "tp"), None),
        P(("groups", "pool", "tp"), None, None),
        P(("groups", "pool", "tp"), None),
        P(("groups", "pool", "tp")),
        P(("groups", "pool"), "tp"),
        P("pool", "tp"),
        P("tp"),
        P("tp", "pool"),
        P("tp", "pool"),
        P("pool", "tp"),
    )
    return jax.shard_map(
        on_device,
        mesh=mesh,
        in_specs=placed,
        out_specs=P(("groups", "pool"), "tp"),
        check_vma=False,
    )
```

```python
import functools
import math
import types

import jax
import jax.numpy as jnp
import numpy as np
from jax import lax
from jax.experimental import pallas as pl
from jax.experimental.pallas import tpu as pltpu
from jax.sharding import PartitionSpec as P

D = 7168
HEADS = 64
HD = 256


epsilon = 1e-06


PAD = 8
LAG = 3
BACK_LAG = 3
SLOTS = 8
CHUNKS = 4
MESH = pl.DeviceIdType.MESH


def tile_of(extent):
    return 256 if extent % 256 == 0 else 128


def sizes_of(pools, tps, amount, places, block, width, cols, ff):
    rows = block * pools
    wide = 256 if ff % 256 == 0 else 384
    parts = 2 if width % 256 == 0 else 1
    pieces = ff // wide
    group = 2 if pieces % 2 == 0 else 1
    return types.SimpleNamespace(
        pools=pools,
        tps=tps,
        chips=pools // 2,
        amount=amount,
        places=places,
        block=block,
        width=width,
        cols=cols,
        ff=ff,
        rows=rows,
        half=rows // 2,
        slab=pools * amount,
        chunk=cols // CHUNKS,
        parts=parts,
        part=width // parts,
        wide=wide,
        low=(wide // 256 * 128 if wide % 256 == 0 else 256, 128),
        pieces=pieces,
        group=group,
        groups=pieces // group,
        turn=max(pieces, pieces // group * (group - 1) + LAG * (tps - 1)),
        slots=min(SLOTS, pieces),
        lanes=-(-rows // 128) * 128,
        out_tile=width // parts if rows <= 256 else tile_of(width // parts),
    )


def scratch_of(z):
    bf16, f32 = jnp.bfloat16, jnp.float32
    dma = pltpu.SemaphoreType.DMA
    vmem = pltpu.VMEM
    held = {
        "cache": vmem((z.amount, z.places, 2 * HD), bf16),
        "flat": vmem((z.amount, z.pools * z.cols), bf16),
        "asked": vmem((2, z.amount, HEADS // 2, HD), f32),
        "mixed": vmem((2, PAD, HEADS // 2, HD), f32),
        "resid": vmem((z.block, z.width), bf16),
        "gain": vmem((z.width,), bf16),
        "pick_local": vmem((z.slab, z.pools * PAD), bf16),
        "pick_all": vmem((z.rows, z.rows), bf16),
        "small_sem": dma((4,)),
        "att": vmem((z.pools, PAD, z.cols), bf16),
        "cache_sem": dma((z.amount,)),
        "flat_sem": dma((1,)),
        "wo": vmem((z.cols, z.width), bf16),
        "wgu": vmem((z.slots, z.width, 2 * z.wide), bf16),
        "wd": vmem((z.ff, z.width), bf16),
        "raw": vmem((z.pools, PAD, z.cols), bf16),
        "slabs": vmem((z.tps, CHUNKS, z.slab, z.chunk), bf16),
        "x": vmem((z.rows, z.chunk), bf16),
        "pf": vmem((z.rows, z.width), f32),
        "pair_out": vmem((z.parts, z.half, z.part), bf16),
        "pair_in": vmem((z.parts, z.half, z.part), bf16),
        "chip_out": vmem((z.parts, z.half, z.part), bf16),
        "chip_in": vmem((z.chips, z.parts, z.half, z.part), bf16),
        "post": vmem((z.half, z.width), f32),
        "own_post": vmem((z.block, z.width), f32),
        "s_in": vmem((z.rows, z.width), bf16),
        "sq_half": vmem((8, z.lanes), f32),
        "sq_pair": vmem((8, z.lanes), f32),
        "sq_all": vmem((z.tps, 8, z.lanes), f32),
        "inv": vmem((z.rows, 128), f32),
        "sums": vmem((z.pieces, z.rows, 2 * z.wide), f32),
        "acc": vmem((z.rows, z.width), f32),
        "end_out": vmem((z.parts, z.half, z.part), bf16),
        "end_in": vmem((z.parts, z.half, z.part), bf16),
        "last_out": vmem((z.chips, z.parts, z.block, z.part), bf16),
        "last_in": vmem((z.chips, z.parts, z.block, z.part), bf16),
        "wo_sem": dma((CHUNKS,)),
        "wd_sem": dma((1,)),
        "g_sem": dma((z.slots,)),
        "u_sem": dma((z.slots,)),
        "a_send": dma((CHUNKS, z.pools)),
        "a_recv": dma((CHUNKS, z.pools)),
        "c_right": dma((z.tps, CHUNKS)),
        "c_left": dma((z.tps, CHUNKS)),
        "c_recv": dma((z.tps, CHUNKS)),
        "pair_send": dma((z.parts,)),
        "pair_recv": dma((z.parts,)),
        "chip_send": dma((z.chips, z.parts)),
        "chip_recv": dma((z.chips, z.parts)),
        "in_send": dma((z.parts,)),
        "in_recv": dma((z.parts,)),
        "sq_send": dma((1,)),
        "sq_recv": dma((1,)),
        "end_send": dma((z.parts,)),
        "end_recv": dma((z.parts,)),
        "last_send": dma((z.chips, z.parts)),
        "last_recv": dma((z.chips, z.parts)),
        "e_send": dma((2,)),
        "e_recv": dma((z.tps,)),
    }
    for s in range(2):
        held["sbuf%d" % s] = vmem((z.pieces, z.rows, 2 * z.low[s]), bf16)
        held["rbuf%d" % s] = vmem((z.pieces, z.rows, 2 * z.low[s]), bf16)
        held["hid%d" % s] = vmem((z.groups, z.group, z.rows, z.low[s]), bf16)
        for name in ("r_send", "r_recv"):
            held["%s%d" % (name, s)] = dma((z.pieces,))
        for name in ("h_send", "h_recv"):
            held["%s%d" % (name, s)] = dma((z.groups,))
    return held


def layer_kernel(
    z,
    names,
    lengths,
    fresh,
    queries_hbm,
    resid_hbm,
    gain_hbm,
    pick_local_hbm,
    pick_all_hbm,
    cache_hbm,
    wo_hbm,
    wg_hbm,
    wu_hbm,
    wd_hbm,
    out,
    *refs,
):
    v = types.SimpleNamespace(**dict(zip(names, refs)))
    att, resid, gain, pick_local, pick_all = v.att, v.resid, v.gain, v.pick_local, v.pick_all
    bf16, f32 = jnp.bfloat16, jnp.float32
    p = lax.axis_index("pool")
    t = lax.axis_index("tp")
    core, chip = lax.rem(p, 2), p // 2
    partner = p + 1 - 2 * core
    last = z.tps - 1
    before, behind = lax.rem(t + z.tps - 1, z.tps), lax.rem(t + 1, z.tps)
    mine = pl.ds(pl.multiple_of(core * z.half, 16), z.half)
    other = pl.ds(pl.multiple_of((1 - core) * z.half, 16), z.half)
    block_in_half = pl.ds(pl.multiple_of(chip * z.block, 8), z.block)
    low_at = (0, z.low[0])

    def span(j, extent):
        return pl.ds(pl.multiple_of(j * extent, 128), extent)

    def wo_copy(k):
        at = pl.ds(pl.multiple_of(k * z.chunk, 128), z.chunk)
        return pltpu.make_async_copy(wo_hbm.at[at], v.wo.at[at], v.wo_sem.at[k])

    def weight_copies(j):
        slot = lax.rem(j, z.slots)
        at = span(j, z.wide)
        return (
            pltpu.make_async_copy(wg_hbm.at[:, at], v.wgu.at[slot, :, pl.ds(0, z.wide)], v.g_sem.at[slot]),
            pltpu.make_async_copy(wu_hbm.at[:, at], v.wgu.at[slot, :, pl.ds(z.wide, z.wide)], v.u_sem.at[slot]),
        )

    wd_copy = pltpu.make_async_copy(wd_hbm, v.wd, v.wd_sem.at[0])

    def remote(src, dst, send, recv, device):
        return pltpu.make_async_remote_copy(
            src_ref=src, dst_ref=dst, send_sem=send, recv_sem=recv, device_id=device, device_id_type=MESH
        )

    def cache_copy(r):
        return pltpu.make_async_copy(cache_hbm.at[r], v.cache.at[r], v.cache_sem.at[r])

    flat_copy = pltpu.make_async_copy(queries_hbm, v.flat, v.flat_sem.at[0])
    flat_copy.start()
    for r in range(z.amount):
        cache_copy(r).start()
    small_copies = [
        pltpu.make_async_copy(src, dst, v.small_sem.at[i])
        for i, (src, dst) in enumerate(
            ((resid_hbm, resid), (gain_hbm, gain), (pick_local_hbm, pick_local), (pick_all_hbm, pick_all))
        )
    ]
    for copy in small_copies:
        copy.start()

    barrier = pltpu.get_barrier_semaphore()
    for k in range(1, z.pools):
        pl.semaphore_signal(barrier, inc=1, device_id={"pool": lax.rem(p + k, z.pools)}, device_id_type=MESH)
    for k in range(1, z.tps):
        pl.semaphore_signal(barrier, inc=1, device_id={"tp": lax.rem(t + k, z.tps)}, device_id_type=MESH)

    def att_copy(j, k):
        q = lax.rem(p + j, z.pools)
        at = pl.ds(k * z.chunk, z.chunk)
        return remote(att.at[q, :, at], v.raw.at[p, :, at], v.a_send.at[k, j], v.a_recv.at[k, p], {"pool": q})

    def att_arrival(j, k):
        q = lax.rem(p + j, z.pools)
        at = pl.ds(k * z.chunk, z.chunk)
        return remote(att.at[q, :, at], v.raw.at[q, :, at], v.a_send.at[k, j], v.a_recv.at[k, q], {"pool": q})


    flat_copy.wait()
    v.mixed[...] = jnp.zeros_like(v.mixed)
    per_block = HEADS // z.pools
    held_heads = per_block // 2

    def attend(part, r):
        factor = 1.0 / math.sqrt(HD)
        heads = v.asked[part, r]
        new_row = fresh[r : r + 1, :].astype(f32)
        scores = (
            lax.dot_general(
                heads.astype(bf16), v.cache[r, :, :HD], (((1,), (1,)), ((), ())), preferred_element_type=f32
            )
            * factor
        )
        own_score = jnp.sum(heads * new_row[:, :HD], axis=1, keepdims=True) * factor
        positions = lax.broadcasted_iota(jnp.int32, scores.shape, 1)
        usable = positions < lengths[r]
        scores = jnp.where(usable, scores, -jnp.inf)
        peak_score = jnp.maximum(jnp.max(scores, axis=1, keepdims=True), own_score)
        weights_raw = jnp.where(usable, jnp.exp(scores - peak_score), 0.0)
        own_raw = jnp.exp(own_score - peak_score)
        share = 1.0 / (jnp.sum(weights_raw, axis=1, keepdims=True) + own_raw)
        weights = (weights_raw * share).astype(bf16)
        own_weight = (own_raw * share).astype(bf16).astype(f32)
        mixture = jnp.dot(weights, v.cache[r, :, HD:], preferred_element_type=f32)
        v.mixed[part, r] = mixture + own_weight * new_row[:, HD:]

    for part in range(2):
        for q in range(z.pools):
            for b in range(held_heads):
                at = (q * per_block + part * held_heads + b) * HD
                v.asked[part, :, q * held_heads + b, :] = v.flat[:, at : at + HD].astype(f32)
        for r in range(z.amount):
            if part == 0 and r % 3 == 0:
                for e in range(r, min(r + 3, z.amount)):
                    cache_copy(e).wait()
            attend(part, r)
        for q in range(z.pools):
            for b in range(held_heads):
                at = pl.ds((part * held_heads + b) * HD, HD)
                v.att[q, :, at] = v.mixed[part, :, q * held_heads + b, :].astype(bf16)
        if part == 0:
            pl.semaphore_wait(barrier, z.pools + z.tps - 2)
        for k in range(part * CHUNKS // 2, (part + 1) * CHUNKS // 2):
            for j in range(1, z.pools):
                att_copy(j, k).start()
    for k in range(CHUNKS):
        wo_copy(k).start()
    for copy in small_copies:
        copy.wait()
    v.raw[p] = att[p]
    v.pf[...] = jnp.zeros_like(v.pf)

    def slab_right(origin, k):
        ref = v.slabs.at[origin, k]
        return remote(ref, ref, v.c_right.at[origin, k], v.c_recv.at[origin, k], {"tp": behind})

    def slab_left(origin, k):
        ref = v.slabs.at[origin, k]
        return remote(ref, ref, v.c_left.at[origin, k], v.c_recv.at[origin, k], {"tp": before})

    for k in range(CHUNKS):
        for j in range(1, z.pools):
            att_arrival(j, k).wait_recv()
        tall = jnp.concatenate([v.raw[q, :, pl.ds(k * z.chunk, z.chunk)].astype(f32) for q in range(z.pools)], axis=0)
        v.slabs[t, k] = jnp.dot(pick_local[...], tall.astype(bf16), preferred_element_type=f32).astype(bf16)

        @pl.when(t < last)
        def _():
            slab_right(t, k).start()

        @pl.when(t > 0)
        def _():
            slab_left(t, k).start()

    for j in range(z.slots):
        for copy in weight_copies(jnp.int32(j)):
            copy.start()
    wd_copy.start()
    def gather_step(d, k):
        @pl.when(t - d >= 0)
        def _():
            slab_left(t - d, k).wait_recv()

            @pl.when(t < last)
            def _():
                slab_right(t - d, k).start()

        @pl.when(t + d <= last)
        def _():
            slab_right(t + d, k).wait_recv()

            @pl.when(t > 0)
            def _():
                slab_left(t + d, k).start()

    for d in range(1, last):
        for k in range(CHUNKS):
            gather_step(d, k)

    def rows_of(k):
        gather_step(last, k)
        tall = jnp.concatenate([v.slabs[o, k].astype(f32) for o in range(z.tps)], axis=0)
        v.x[...] = jnp.dot(pick_all[...], tall.astype(bf16), preferred_element_type=f32).astype(bf16)
        wo_copy(k).wait()

    def project(k, at):
        down_rows = pl.ds(pl.multiple_of(k * z.chunk, 128), z.chunk)
        v.pf[:, at] += jnp.dot(v.x[...], v.wo[down_rows, at], preferred_element_type=f32)

    @pl.loop(0, CHUNKS - 1)
    def _(k):
        rows_of(k)

        @pl.loop(0, z.width // z.out_tile)
        def _(n):
            project(k, span(n, z.out_tile))

    def pair_copy(n):
        return remote(
            v.pair_out.at[n], v.pair_in.at[n], v.pair_send.at[n], v.pair_recv.at[n], {"pool": partner}
        )

    def chip_copy(j, n):
        to = lax.rem(chip + j, z.chips)
        return remote(
            v.chip_out.at[n], v.chip_in.at[chip, n], v.chip_send.at[j, n], v.chip_recv.at[chip, n], {"pool": 2 * to + core}
        )

    def chip_arrival(j, n):
        to = lax.rem(chip + j, z.chips)
        return remote(
            v.chip_out.at[n], v.chip_in.at[to, n], v.chip_send.at[j, n], v.chip_recv.at[to, n], {"pool": 2 * to + core}
        )

    def in_copy(n):
        ref = v.s_in.at[mine, pl.ds(n * z.part, z.part)]
        return remote(ref, ref, v.in_send.at[n], v.in_recv.at[n], {"pool": partner})

    def in_arrival(n):
        ref = v.s_in.at[other, pl.ds(n * z.part, z.part)]
        return remote(ref, ref, v.in_send.at[n], v.in_recv.at[n], {"pool": partner})

    sq_copy = remote(v.sq_half, v.sq_pair, v.sq_send.at[0], v.sq_recv.at[0], {"pool": partner})

    rows_of(CHUNKS - 1)
    for n in range(z.parts):
        at = pl.ds(n * z.part, z.part)

        @pl.loop(0, z.part // z.out_tile)
        def _(m):
            project(CHUNKS - 1, pl.ds(pl.multiple_of(n * z.part + m * z.out_tile, 128), z.out_tile))

        v.pair_out[n] = v.pf[other, at].astype(bf16)
        pair_copy(n).start()

    for n in range(z.parts):
        at = pl.ds(n * z.part, z.part)
        pair_copy(n).wait_recv()
        v.post[:, at] = v.pf[mine, at] + v.pair_in[n].astype(f32)
        v.post[block_in_half, at] += resid[:, at].astype(f32)
        v.chip_out[n] = v.post[:, at].astype(bf16)
        for j in range(1, z.chips):
            chip_copy(j, n).start()

    squares = jnp.zeros((z.half, 1), f32)
    for n in range(z.parts):
        at = pl.ds(n * z.part, z.part)
        value = v.post[:, at]
        for j in range(1, z.chips):
            chip_arrival(j, n).wait_recv()
            value = value + v.chip_in[lax.rem(chip + j, z.chips), n].astype(f32)
        v.post[:, at] = value
        v.s_in[mine, at] = (value * gain[at].astype(f32)[None, :]).astype(bf16)
        in_copy(n).start()
        squares = squares + jnp.sum(value * value, axis=1, keepdims=True)

    lane = lax.broadcasted_iota(jnp.int32, (z.half, z.lanes), 1)
    row = lax.broadcasted_iota(jnp.int32, (z.half, z.lanes), 0) + core * z.half
    flat = jnp.sum(jnp.where(lane == row, squares, 0.0), axis=0, keepdims=True)
    v.sq_half[...] = jnp.broadcast_to(flat, (8, z.lanes))
    sq_copy.start()
    v.own_post[...] = v.post[block_in_half, :]
    v.acc[...] = jnp.zeros_like(v.acc)
    for n in range(z.parts):
        in_arrival(n).wait_recv()
    sq_copy.wait_recv()
    v.sq_all[t] = v.sq_half[...] + v.sq_pair[...]

    ends = (0, last)

    def square_copy(s):
        return remote(v.sq_all.at[t], v.sq_all.at[t], v.e_send.at[s], v.e_recv.at[t], {"tp": ends[s]})

    def square_arrival(o):
        return remote(v.sq_all.at[o], v.sq_all.at[o], v.e_send.at[0], v.e_recv.at[o], {"tp": o})

    for s in range(2):

        @pl.when(t != ends[s])
        def _():
            square_copy(s).start()

    def scale_rows():
        for o in range(z.tps):

            @pl.when(t != o)
            def _():
                square_arrival(o).wait_recv()

        total = v.sq_all[0]
        for o in range(1, z.tps):
            total = total + v.sq_all[o]
        lane = lax.broadcasted_iota(jnp.int32, (z.rows, z.lanes), 1)
        row = lax.broadcasted_iota(jnp.int32, (z.rows, z.lanes), 0)
        tall = jnp.sum(jnp.where(lane == row, total[0:1], 0.0), axis=1, keepdims=True)
        v.inv[...] = jnp.broadcast_to(lax.rsqrt(tall / D + epsilon), (z.rows, 128))

    hid = (v.hid0, v.hid1)
    sbuf, rbuf = (v.sbuf0, v.sbuf1), (v.rbuf0, v.rbuf1)
    r_send, r_recv = (v.r_send0, v.r_send1), (v.r_recv0, v.r_recv1)
    h_send, h_recv = (v.h_send0, v.h_send1), (v.h_recv0, v.h_recv1)

    def lanes(s):
        if s == 0:
            return last - t, before, behind
        return t, behind, before

    def sum_hop(s, j):
        return remote(sbuf[s].at[j], rbuf[s].at[j], r_send[s].at[j], r_recv[s].at[j], {"tp": lanes(s)[1]})

    def hidden_hop(s, j):
        return remote(hid[s].at[j], hid[s].at[j], h_send[s].at[j], h_recv[s].at[j], {"tp": lanes(s)[2]})

    def compute(j):
        for copy in weight_copies(j):
            copy.wait()
        v.sums[j] = jnp.dot(v.s_in[...], v.wgu[lax.rem(j, z.slots)], preferred_element_type=f32)

        @pl.when(j + z.slots < z.pieces)
        def _():
            for copy in weight_copies(j + z.slots):
                copy.start()

    def down(g, at):
        held = [hid[s][g, b] for b in range(z.group) for s in range(2)]
        extent = z.group * z.wide
        v.acc[:, at] += jnp.dot(
            jnp.concatenate(held, axis=1),
            v.wd[pl.ds(pl.multiple_of(g * extent, 128), extent), at],
            preferred_element_type=f32,
        )

    wd_copy.wait()
    compute(jnp.int32(0))
    def one_step(i):
        for s in range(2):
            far, _, _ = lanes(s)
            c = i - LAG * far
            at_gate = pl.ds(low_at[s], z.low[s])
            at_up = pl.ds(z.wide + low_at[s], z.low[s])

            def summed():
                gate = v.sums[c, :, at_gate] + rbuf[s][c, :, : z.low[s]].astype(f32)
                return gate, v.sums[c, :, at_up] + rbuf[s][c, :, z.low[s] :].astype(f32)

            def pass_on(gate, up):
                sbuf[s][c, :, : z.low[s]] = gate.astype(bf16)
                sbuf[s][c, :, z.low[s] :] = up.astype(bf16)
                sum_hop(s, c).start()

            inside = (c >= 0) & (c < z.pieces)

            @pl.when(inside & (far == 0))
            def _():
                pass_on(v.sums[c, :, at_gate], v.sums[c, :, at_up])

            @pl.when(inside & (far > 0) & (far < last))
            def _():
                sum_hop(s, c).wait_recv()
                pass_on(*summed())

            @pl.when(inside & (far == last))
            def _():
                @pl.when(c == 0)
                def _():
                    scale_rows()

                sum_hop(s, c).wait_recv()
                inv = v.inv[:, :1]
                gate, up = summed()
                gate, up = gate * inv, up * inv
                hid[s][lax.div(c, z.group), lax.rem(c, z.group)] = (gate / (1.0 + jnp.exp(-gate)) * up).astype(bf16)

        for s in range(2):
            far, _, _ = lanes(s)
            back = last - far
            g = i - z.turn - BACK_LAG * back

            @pl.when((g >= 0) & (g < z.groups))
            def _():
                @pl.when(back > 0)
                def _():
                    hidden_hop(s, g).wait_recv()

                @pl.when(back < last)
                def _():
                    hidden_hop(s, g).start()

        @pl.when(i + 1 < z.pieces)
        def _():
            compute(i + 1)

        g = i - z.turn - BACK_LAG * jnp.maximum(t, last - t)

        @pl.when((g >= 0) & (g < z.groups - 1))
        def _():
            @pl.loop(0, z.width // z.out_tile)
            def _(n):
                down(g, span(n, z.out_tile))

    pl.loop(0, z.turn + z.groups + BACK_LAG * last)(one_step)

    def end_copy(n):
        return remote(v.end_out.at[n], v.end_in.at[n], v.end_send.at[n], v.end_recv.at[n], {"pool": partner})

    def last_copy(j, n):
        to = lax.rem(chip + j, z.chips)
        return remote(
            v.last_out.at[to, n], v.last_in.at[chip, n], v.last_send.at[j, n], v.last_recv.at[chip, n], {"pool": 2 * to + core}
        )

    def last_arrival(j, n):
        to = lax.rem(chip + j, z.chips)
        return remote(
            v.last_out.at[to, n], v.last_in.at[to, n], v.last_send.at[j, n], v.last_recv.at[to, n], {"pool": 2 * to + core}
        )

    for n in range(z.parts):

        @pl.loop(0, z.part // z.out_tile)
        def _(m):
            down(z.groups - 1, pl.ds(pl.multiple_of(n * z.part + m * z.out_tile, 128), z.out_tile))

        v.end_out[n] = v.acc[other, pl.ds(n * z.part, z.part)].astype(bf16)
        end_copy(n).start()
    for j in range(1, z.pools):
        for k in range(CHUNKS):
            att_copy(j, k).wait_send()
    for n in range(z.parts):
        pair_copy(n).wait_send()
        in_copy(n).wait_send()
        for j in range(1, z.chips):
            chip_copy(j, n).wait_send()
    sq_copy.wait_send()
    for s in range(2):

        @pl.when(t != ends[s])
        def _():
            square_copy(s).wait_send()

    @pl.loop(0, CHUNKS)
    def _(k):
        for origin in range(z.tps):

            @pl.when((t < last) & (origin <= t))
            def _():
                slab_right(origin, k).wait_send()

            @pl.when((t > 0) & (origin >= t))
            def _():
                slab_left(origin, k).wait_send()

    for n in range(z.parts):
        at = pl.ds(n * z.part, z.part)
        end_copy(n).wait_recv()
        v.post[:, at] = v.acc[mine, at] + v.end_in[n].astype(f32)
        for q in range(z.chips):
            v.last_out[q, n] = v.post[pl.ds(q * z.block, z.block), at].astype(bf16)
        for j in range(1, z.chips):
            last_copy(j, n).start()
    @pl.loop(0, z.pieces)
    def _(c):
        for s in range(2):
            far, _, _ = lanes(s)

            @pl.when(far < last)
            def _():
                sum_hop(s, c).wait_send()

            @pl.when((far > 0) & (c < z.groups))
            def _():
                hidden_hop(s, c).wait_send()
    for n in range(z.parts):
        at = pl.ds(n * z.part, z.part)
        total = v.own_post[:, at] + v.post[block_in_half, at]
        for j in range(1, z.chips):
            last_arrival(j, n).wait_recv()
            total = total + v.last_in[lax.rem(chip + j, z.chips), n].astype(f32)
        out[:, at] = total.astype(bf16)

    for n in range(z.parts):
        end_copy(n).wait_send()
        for j in range(1, z.chips):
            last_copy(j, n).wait_send()


def on_device(
    queries,
    cached_entries,
    new_entry,
    lengths,
    residual,
    out_weight,
    norm_gain,
    gate_weight,
    up_weight,
    down_weight,
):
    pools, tps = lax.axis_size("pool"), lax.axis_size("tp")
    amount, cols = queries.shape[0], queries.shape[1] // pools
    block, width = residual.shape
    z = sizes_of(pools, tps, amount, cached_entries.shape[1], block, width, cols, gate_weight.shape[1])

    local = np.arange(z.slab)
    pick_local = np.zeros((z.slab, pools * PAD), np.float32)
    pick_local[local, local // amount * PAD + local % amount] = 1
    every = np.arange(z.rows)
    of_core, of_chip = every // z.half, every % z.half // block
    of_tp, of_row = every // amount % tps, every % amount
    pick_all = np.zeros((z.rows, z.rows), np.float32)
    pick_all[every, (of_tp * pools + 2 * of_chip + of_core) * amount + of_row] = 1

    vmem = pl.BlockSpec(memory_space=pltpu.VMEM)
    anywhere = pl.BlockSpec(memory_space=pl.ANY)
    bf16 = jnp.bfloat16
    held = scratch_of(z)
    return pl.pallas_call(
        functools.partial(layer_kernel, z, tuple(held)),
        out_shape=jax.ShapeDtypeStruct((block, width), bf16),
        in_specs=[pl.BlockSpec(memory_space=pltpu.SMEM), vmem] + [anywhere] * 10,
        out_specs=vmem,
        scratch_shapes=list(held.values()),
        compiler_params=pltpu.CompilerParams(
            collective_id=0, has_side_effects=True, vmem_limit_bytes=62 << 20
        ),
        name="layer",
    )(
        lengths,
        new_entry,
        queries,
        residual,
        norm_gain,
        jnp.asarray(pick_local, bf16),
        jnp.asarray(pick_all, bf16),
        cached_entries,
        out_weight,
        gate_weight,
        up_weight,
        down_weight,
    )


def solution(mesh):
    placed = (
        P(("groups", "pool", "tp"), None),
        P(("groups", "pool", "tp"), None, None),
        P(("groups", "pool", "tp"), None),
        P(("groups", "pool", "tp")),
        P(("groups", "pool"), "tp"),
        P("pool", "tp"),
        P("tp"),
        P("tp", "pool"),
        P("tp", "pool"),
        P("pool", "tp"),
    )
    return jax.shard_map(
        on_device,
        mesh=mesh,
        in_specs=placed,
        out_specs=P(("groups", "pool"), "tp"),
        check_vma=False,
    )
```

```python
import functools
import math
import types

import jax
import jax.numpy as jnp
import numpy as np
from jax import lax
from jax.experimental import pallas as pl
from jax.experimental.pallas import tpu as pltpu
from jax.sharding import PartitionSpec as P

D = 7168
HEADS = 64
HD = 256


epsilon = 1e-06


PAD = 8
LAG = 4
BACK_LAG = 4
SLOTS = 8
CHUNKS = 4
MESH = pl.DeviceIdType.MESH


def tile_of(extent):
    return 256 if extent % 256 == 0 else 128


def sizes_of(pools, tps, amount, places, block, width, cols, ff):
    rows = block * pools
    wide = 256 if ff % 256 == 0 else 384
    parts = 2 if width % 256 == 0 else 1
    pieces = ff // wide
    group = 2 if pieces % 2 == 0 else 1
    return types.SimpleNamespace(
        pools=pools,
        tps=tps,
        chips=pools // 2,
        amount=amount,
        places=places,
        block=block,
        width=width,
        cols=cols,
        ff=ff,
        rows=rows,
        half=rows // 2,
        slab=pools * amount,
        chunk=cols // CHUNKS,
        parts=parts,
        part=width // parts,
        wide=wide,
        low=(wide // 256 * 128 if wide % 256 == 0 else 256, 128),
        pieces=pieces,
        group=group,
        groups=pieces // group,
        turn=max(pieces, pieces // group * (group - 1) + LAG * (tps - 1)),
        slots=min(SLOTS, pieces),
        lanes=-(-rows // 128) * 128,
        out_tile=width // parts if rows <= 256 else tile_of(width // parts),
    )


def scratch_of(z):
    bf16, f32 = jnp.bfloat16, jnp.float32
    dma = pltpu.SemaphoreType.DMA
    vmem = pltpu.VMEM
    held = {
        "cache": vmem((z.amount, z.places, 2 * HD), bf16),
        "flat": vmem((z.amount, z.pools * z.cols), bf16),
        "asked": vmem((2, z.amount, HEADS // 2, HD), f32),
        "mixed": vmem((2, PAD, HEADS // 2, HD), f32),
        "resid": vmem((z.block, z.width), bf16),
        "gain": vmem((z.width,), bf16),
        "pick_local": vmem((z.slab, z.pools * PAD), bf16),
        "pick_all": vmem((z.rows, z.rows), bf16),
        "small_sem": dma((4,)),
        "att": vmem((z.pools, PAD, z.cols), bf16),
        "cache_sem": dma((z.amount,)),
        "flat_sem": dma((1,)),
        "wo": vmem((z.cols, z.width), bf16),
        "wgu": vmem((z.slots, z.width, 2 * z.wide), bf16),
        "wd": vmem((z.ff, z.width), bf16),
        "raw": vmem((z.pools, PAD, z.cols), bf16),
        "slabs": vmem((z.tps, CHUNKS, z.slab, z.chunk), bf16),
        "x": vmem((z.rows, z.chunk), bf16),
        "pf": vmem((z.rows, z.width), f32),
        "pair_out": vmem((z.parts, z.half, z.part), bf16),
        "pair_in": vmem((z.parts, z.half, z.part), bf16),
        "chip_out": vmem((z.parts, z.half, z.part), bf16),
        "chip_in": vmem((z.chips, z.parts, z.half, z.part), bf16),
        "post": vmem((z.half, z.width), f32),
        "own_post": vmem((z.block, z.width), f32),
        "s_in": vmem((z.rows, z.width), bf16),
        "sq_half": vmem((8, z.lanes), f32),
        "sq_pair": vmem((8, z.lanes), f32),
        "sq_all": vmem((z.tps, 8, z.lanes), f32),
        "inv": vmem((z.rows, 128), f32),
        "sums": vmem((z.pieces, z.rows, 2 * z.wide), f32),
        "acc": vmem((z.rows, z.width), f32),
        "end_out": vmem((z.parts, z.half, z.part), bf16),
        "end_in": vmem((z.parts, z.half, z.part), bf16),
        "last_out": vmem((z.chips, z.parts, z.block, z.part), bf16),
        "last_in": vmem((z.chips, z.parts, z.block, z.part), bf16),
        "wo_sem": dma((CHUNKS,)),
        "wd_sem": dma((1,)),
        "g_sem": dma((z.slots,)),
        "u_sem": dma((z.slots,)),
        "a_send": dma((CHUNKS, z.pools)),
        "a_recv": dma((CHUNKS, z.pools)),
        "c_right": dma((z.tps, CHUNKS)),
        "c_left": dma((z.tps, CHUNKS)),
        "c_recv": dma((z.tps, CHUNKS)),
        "pair_send": dma((z.parts,)),
        "pair_recv": dma((z.parts,)),
        "chip_send": dma((z.chips, z.parts)),
        "chip_recv": dma((z.chips, z.parts)),
        "in_send": dma((z.parts,)),
        "in_recv": dma((z.parts,)),
        "sq_send": dma((1,)),
        "sq_recv": dma((1,)),
        "end_send": dma((z.parts,)),
        "end_recv": dma((z.parts,)),
        "last_send": dma((z.chips, z.parts)),
        "last_recv": dma((z.chips, z.parts)),
        "e_send": dma((2,)),
        "e_recv": dma((z.tps,)),
    }
    for s in range(2):
        held["sbuf%d" % s] = vmem((z.pieces, z.rows, 2 * z.low[s]), bf16)
        held["rbuf%d" % s] = vmem((z.pieces, z.rows, 2 * z.low[s]), bf16)
        held["hid%d" % s] = vmem((z.groups, z.group, z.rows, z.low[s]), bf16)
        for name in ("r_send", "r_recv"):
            held["%s%d" % (name, s)] = dma((z.pieces,))
        for name in ("h_send", "h_recv"):
            held["%s%d" % (name, s)] = dma((z.groups,))
    return held


def layer_kernel(
    z,
    names,
    lengths,
    fresh,
    queries_hbm,
    resid_hbm,
    gain_hbm,
    pick_local_hbm,
    pick_all_hbm,
    cache_hbm,
    wo_hbm,
    wg_hbm,
    wu_hbm,
    wd_hbm,
    out,
    *refs,
):
    v = types.SimpleNamespace(**dict(zip(names, refs)))
    att, resid, gain, pick_local, pick_all = v.att, v.resid, v.gain, v.pick_local, v.pick_all
    bf16, f32 = jnp.bfloat16, jnp.float32
    p = lax.axis_index("pool")
    t = lax.axis_index("tp")
    core, chip = lax.rem(p, 2), p // 2
    partner = p + 1 - 2 * core
    last = z.tps - 1
    before, behind = lax.rem(t + z.tps - 1, z.tps), lax.rem(t + 1, z.tps)
    mine = pl.ds(pl.multiple_of(core * z.half, 16), z.half)
    other = pl.ds(pl.multiple_of((1 - core) * z.half, 16), z.half)
    block_in_half = pl.ds(pl.multiple_of(chip * z.block, 8), z.block)
    low_at = (0, z.low[0])

    def span(j, extent):
        return pl.ds(pl.multiple_of(j * extent, 128), extent)

    def wo_copy(k):
        at = pl.ds(pl.multiple_of(k * z.chunk, 128), z.chunk)
        return pltpu.make_async_copy(wo_hbm.at[at], v.wo.at[at], v.wo_sem.at[k])

    def weight_copies(j):
        slot = lax.rem(j, z.slots)
        at = span(j, z.wide)
        return (
            pltpu.make_async_copy(wg_hbm.at[:, at], v.wgu.at[slot, :, pl.ds(0, z.wide)], v.g_sem.at[slot]),
            pltpu.make_async_copy(wu_hbm.at[:, at], v.wgu.at[slot, :, pl.ds(z.wide, z.wide)], v.u_sem.at[slot]),
        )

    wd_copy = pltpu.make_async_copy(wd_hbm, v.wd, v.wd_sem.at[0])

    def remote(src, dst, send, recv, device):
        return pltpu.make_async_remote_copy(
            src_ref=src, dst_ref=dst, send_sem=send, recv_sem=recv, device_id=device, device_id_type=MESH
        )

    def cache_copy(r):
        return pltpu.make_async_copy(cache_hbm.at[r], v.cache.at[r], v.cache_sem.at[r])

    flat_copy = pltpu.make_async_copy(queries_hbm, v.flat, v.flat_sem.at[0])
    flat_copy.start()
    for r in range(z.amount):
        cache_copy(r).start()
    small_copies = [
        pltpu.make_async_copy(src, dst, v.small_sem.at[i])
        for i, (src, dst) in enumerate(
            ((resid_hbm, resid), (gain_hbm, gain), (pick_local_hbm, pick_local), (pick_all_hbm, pick_all))
        )
    ]
    for copy in small_copies:
        copy.start()

    barrier = pltpu.get_barrier_semaphore()
    for k in range(1, z.pools):
        pl.semaphore_signal(barrier, inc=1, device_id={"pool": lax.rem(p + k, z.pools)}, device_id_type=MESH)
    for k in range(1, z.tps):
        pl.semaphore_signal(barrier, inc=1, device_id={"tp": lax.rem(t + k, z.tps)}, device_id_type=MESH)

    def att_copy(j, k):
        q = lax.rem(p + j, z.pools)
        at = pl.ds(k * z.chunk, z.chunk)
        return remote(att.at[q, :, at], v.raw.at[p, :, at], v.a_send.at[k, j], v.a_recv.at[k, p], {"pool": q})

    def att_arrival(j, k):
        q = lax.rem(p + j, z.pools)
        at = pl.ds(k * z.chunk, z.chunk)
        return remote(att.at[q, :, at], v.raw.at[q, :, at], v.a_send.at[k, j], v.a_recv.at[k, q], {"pool": q})


    flat_copy.wait()
    v.mixed[...] = jnp.zeros_like(v.mixed)
    per_block = HEADS // z.pools
    held_heads = per_block // 2

    def attend(part, r):
        factor = 1.0 / math.sqrt(HD)
        heads = v.asked[part, r]
        new_row = fresh[r : r + 1, :].astype(f32)
        scores = (
            lax.dot_general(
                heads.astype(bf16), v.cache[r, :, :HD], (((1,), (1,)), ((), ())), preferred_element_type=f32
            )
            * factor
        )
        own_score = jnp.sum(heads * new_row[:, :HD], axis=1, keepdims=True) * factor
        positions = lax.broadcasted_iota(jnp.int32, scores.shape, 1)
        usable = positions < lengths[r]
        scores = jnp.where(usable, scores, -jnp.inf)
        peak_score = jnp.maximum(jnp.max(scores, axis=1, keepdims=True), own_score)
        weights_raw = jnp.where(usable, jnp.exp(scores - peak_score), 0.0)
        own_raw = jnp.exp(own_score - peak_score)
        share = 1.0 / (jnp.sum(weights_raw, axis=1, keepdims=True) + own_raw)
        weights = (weights_raw * share).astype(bf16)
        own_weight = (own_raw * share).astype(bf16).astype(f32)
        mixture = jnp.dot(weights, v.cache[r, :, HD:], preferred_element_type=f32)
        v.mixed[part, r] = mixture + own_weight * new_row[:, HD:]

    for part in range(2):
        for q in range(z.pools):
            for b in range(held_heads):
                at = (q * per_block + part * held_heads + b) * HD
                v.asked[part, :, q * held_heads + b, :] = v.flat[:, at : at + HD].astype(f32)
        for r in range(z.amount):
            if part == 0 and r % 3 == 0:
                for e in range(r, min(r + 3, z.amount)):
                    cache_copy(e).wait()
            attend(part, r)
        for q in range(z.pools):
            for b in range(held_heads):
                at = pl.ds((part * held_heads + b) * HD, HD)
                v.att[q, :, at] = v.mixed[part, :, q * held_heads + b, :].astype(bf16)
        if part == 0:
            pl.semaphore_wait(barrier, z.pools + z.tps - 2)
        for k in range(part * CHUNKS // 2, (part + 1) * CHUNKS // 2):
            for j in range(1, z.pools):
                att_copy(j, k).start()
    for k in range(CHUNKS):
        wo_copy(k).start()
    for copy in small_copies:
        copy.wait()
    v.raw[p] = att[p]
    v.pf[...] = jnp.zeros_like(v.pf)

    def slab_right(origin, k):
        ref = v.slabs.at[origin, k]
        return remote(ref, ref, v.c_right.at[origin, k], v.c_recv.at[origin, k], {"tp": behind})

    def slab_left(origin, k):
        ref = v.slabs.at[origin, k]
        return remote(ref, ref, v.c_left.at[origin, k], v.c_recv.at[origin, k], {"tp": before})

    for k in range(CHUNKS):
        for j in range(1, z.pools):
            att_arrival(j, k).wait_recv()
        tall = jnp.concatenate([v.raw[q, :, pl.ds(k * z.chunk, z.chunk)].astype(f32) for q in range(z.pools)], axis=0)
        v.slabs[t, k] = jnp.dot(pick_local[...], tall.astype(bf16), preferred_element_type=f32).astype(bf16)

        @pl.when(t < last)
        def _():
            slab_right(t, k).start()

        @pl.when(t > 0)
        def _():
            slab_left(t, k).start()

    for j in range(z.slots):
        for copy in weight_copies(jnp.int32(j)):
            copy.start()
    wd_copy.start()
    def gather_step(d, k):
        @pl.when(t - d >= 0)
        def _():
            slab_left(t - d, k).wait_recv()

            @pl.when(t < last)
            def _():
                slab_right(t - d, k).start()

        @pl.when(t + d <= last)
        def _():
            slab_right(t + d, k).wait_recv()

            @pl.when(t > 0)
            def _():
                slab_left(t + d, k).start()

    for d in range(1, last):
        for k in range(CHUNKS):
            gather_step(d, k)

    def rows_of(k):
        gather_step(last, k)
        tall = jnp.concatenate([v.slabs[o, k].astype(f32) for o in range(z.tps)], axis=0)
        v.x[...] = jnp.dot(pick_all[...], tall.astype(bf16), preferred_element_type=f32).astype(bf16)
        wo_copy(k).wait()

    def project(k, at):
        down_rows = pl.ds(pl.multiple_of(k * z.chunk, 128), z.chunk)
        v.pf[:, at] += jnp.dot(v.x[...], v.wo[down_rows, at], preferred_element_type=f32)

    @pl.loop(0, CHUNKS - 1)
    def _(k):
        rows_of(k)

        @pl.loop(0, z.width // z.out_tile)
        def _(n):
            project(k, span(n, z.out_tile))

    def pair_copy(n):
        return remote(
            v.pair_out.at[n], v.pair_in.at[n], v.pair_send.at[n], v.pair_recv.at[n], {"pool": partner}
        )

    def chip_copy(j, n):
        to = lax.rem(chip + j, z.chips)
        return remote(
            v.chip_out.at[n], v.chip_in.at[chip, n], v.chip_send.at[j, n], v.chip_recv.at[chip, n], {"pool": 2 * to + core}
        )

    def chip_arrival(j, n):
        to = lax.rem(chip + j, z.chips)
        return remote(
            v.chip_out.at[n], v.chip_in.at[to, n], v.chip_send.at[j, n], v.chip_recv.at[to, n], {"pool": 2 * to + core}
        )

    def in_copy(n):
        ref = v.s_in.at[mine, pl.ds(n * z.part, z.part)]
        return remote(ref, ref, v.in_send.at[n], v.in_recv.at[n], {"pool": partner})

    def in_arrival(n):
        ref = v.s_in.at[other, pl.ds(n * z.part, z.part)]
        return remote(ref, ref, v.in_send.at[n], v.in_recv.at[n], {"pool": partner})

    sq_copy = remote(v.sq_half, v.sq_pair, v.sq_send.at[0], v.sq_recv.at[0], {"pool": partner})

    rows_of(CHUNKS - 1)
    for n in range(z.parts):
        at = pl.ds(n * z.part, z.part)

        @pl.loop(0, z.part // z.out_tile)
        def _(m):
            project(CHUNKS - 1, pl.ds(pl.multiple_of(n * z.part + m * z.out_tile, 128), z.out_tile))

        v.pair_out[n] = v.pf[other, at].astype(bf16)
        pair_copy(n).start()

    for n in range(z.parts):
        at = pl.ds(n * z.part, z.part)
        pair_copy(n).wait_recv()
        v.post[:, at] = v.pf[mine, at] + v.pair_in[n].astype(f32)
        v.post[block_in_half, at] += resid[:, at].astype(f32)
        v.chip_out[n] = v.post[:, at].astype(bf16)
        for j in range(1, z.chips):
            chip_copy(j, n).start()

    squares = jnp.zeros((z.half, 1), f32)
    for n in range(z.parts):
        at = pl.ds(n * z.part, z.part)
        value = v.post[:, at]
        for j in range(1, z.chips):
            chip_arrival(j, n).wait_recv()
            value = value + v.chip_in[lax.rem(chip + j, z.chips), n].astype(f32)
        v.post[:, at] = value
        v.s_in[mine, at] = (value * gain[at].astype(f32)[None, :]).astype(bf16)
        in_copy(n).start()
        squares = squares + jnp.sum(value * value, axis=1, keepdims=True)

    lane = lax.broadcasted_iota(jnp.int32, (z.half, z.lanes), 1)
    row = lax.broadcasted_iota(jnp.int32, (z.half, z.lanes), 0) + core * z.half
    flat = jnp.sum(jnp.where(lane == row, squares, 0.0), axis=0, keepdims=True)
    v.sq_half[...] = jnp.broadcast_to(flat, (8, z.lanes))
    sq_copy.start()
    v.own_post[...] = v.post[block_in_half, :]
    v.acc[...] = jnp.zeros_like(v.acc)
    for n in range(z.parts):
        in_arrival(n).wait_recv()
    sq_copy.wait_recv()
    v.sq_all[t] = v.sq_half[...] + v.sq_pair[...]

    ends = (0, last)

    def square_copy(s):
        return remote(v.sq_all.at[t], v.sq_all.at[t], v.e_send.at[s], v.e_recv.at[t], {"tp": ends[s]})

    def square_arrival(o):
        return remote(v.sq_all.at[o], v.sq_all.at[o], v.e_send.at[0], v.e_recv.at[o], {"tp": o})

    for s in range(2):

        @pl.when(t != ends[s])
        def _():
            square_copy(s).start()

    def scale_rows():
        for o in range(z.tps):

            @pl.when(t != o)
            def _():
                square_arrival(o).wait_recv()

        total = v.sq_all[0]
        for o in range(1, z.tps):
            total = total + v.sq_all[o]
        lane = lax.broadcasted_iota(jnp.int32, (z.rows, z.lanes), 1)
        row = lax.broadcasted_iota(jnp.int32, (z.rows, z.lanes), 0)
        tall = jnp.sum(jnp.where(lane == row, total[0:1], 0.0), axis=1, keepdims=True)
        v.inv[...] = jnp.broadcast_to(lax.rsqrt(tall / D + epsilon), (z.rows, 128))

    hid = (v.hid0, v.hid1)
    sbuf, rbuf = (v.sbuf0, v.sbuf1), (v.rbuf0, v.rbuf1)
    r_send, r_recv = (v.r_send0, v.r_send1), (v.r_recv0, v.r_recv1)
    h_send, h_recv = (v.h_send0, v.h_send1), (v.h_recv0, v.h_recv1)

    def lanes(s):
        if s == 0:
            return last - t, before, behind
        return t, behind, before

    def sum_hop(s, j):
        return remote(sbuf[s].at[j], rbuf[s].at[j], r_send[s].at[j], r_recv[s].at[j], {"tp": lanes(s)[1]})

    def hidden_hop(s, j):
        return remote(hid[s].at[j], hid[s].at[j], h_send[s].at[j], h_recv[s].at[j], {"tp": lanes(s)[2]})

    def compute(j):
        for copy in weight_copies(j):
            copy.wait()
        v.sums[j] = jnp.dot(v.s_in[...], v.wgu[lax.rem(j, z.slots)], preferred_element_type=f32)

        @pl.when(j + z.slots < z.pieces)
        def _():
            for copy in weight_copies(j + z.slots):
                copy.start()

    def down(g, at):
        held = [hid[s][g, b] for b in range(z.group) for s in range(2)]
        extent = z.group * z.wide
        v.acc[:, at] += jnp.dot(
            jnp.concatenate(held, axis=1),
            v.wd[pl.ds(pl.multiple_of(g * extent, 128), extent), at],
            preferred_element_type=f32,
        )

    wd_copy.wait()
    compute(jnp.int32(0))
    def one_step(i):
        for s in range(2):
            far, _, _ = lanes(s)
            c = i - LAG * far
            at_gate = pl.ds(low_at[s], z.low[s])
            at_up = pl.ds(z.wide + low_at[s], z.low[s])

            def summed():
                gate = v.sums[c, :, at_gate] + rbuf[s][c, :, : z.low[s]].astype(f32)
                return gate, v.sums[c, :, at_up] + rbuf[s][c, :, z.low[s] :].astype(f32)

            def pass_on(gate, up):
                sbuf[s][c, :, : z.low[s]] = gate.astype(bf16)
                sbuf[s][c, :, z.low[s] :] = up.astype(bf16)
                sum_hop(s, c).start()

            inside = (c >= 0) & (c < z.pieces)

            @pl.when(inside & (far == 0))
            def _():
                pass_on(v.sums[c, :, at_gate], v.sums[c, :, at_up])

            @pl.when(inside & (far > 0) & (far < last))
            def _():
                sum_hop(s, c).wait_recv()
                pass_on(*summed())

            @pl.when(inside & (far == last))
            def _():
                @pl.when(c == 0)
                def _():
                    scale_rows()

                sum_hop(s, c).wait_recv()
                inv = v.inv[:, :1]
                gate, up = summed()
                gate, up = gate * inv, up * inv
                hid[s][lax.div(c, z.group), lax.rem(c, z.group)] = (gate / (1.0 + jnp.exp(-gate)) * up).astype(bf16)

        for s in range(2):
            far, _, _ = lanes(s)
            back = last - far
            g = i - z.turn - BACK_LAG * back

            @pl.when((g >= 0) & (g < z.groups))
            def _():
                @pl.when(back > 0)
                def _():
                    hidden_hop(s, g).wait_recv()

                @pl.when(back < last)
                def _():
                    hidden_hop(s, g).start()

        @pl.when(i + 1 < z.pieces)
        def _():
            compute(i + 1)

        g = i - z.turn - BACK_LAG * jnp.maximum(t, last - t)

        @pl.when((g >= 0) & (g < z.groups - 1))
        def _():
            @pl.loop(0, z.width // z.out_tile)
            def _(n):
                down(g, span(n, z.out_tile))

    pl.loop(0, z.turn + z.groups + BACK_LAG * last)(one_step)

    def end_copy(n):
        return remote(v.end_out.at[n], v.end_in.at[n], v.end_send.at[n], v.end_recv.at[n], {"pool": partner})

    def last_copy(j, n):
        to = lax.rem(chip + j, z.chips)
        return remote(
            v.last_out.at[to, n], v.last_in.at[chip, n], v.last_send.at[j, n], v.last_recv.at[chip, n], {"pool": 2 * to + core}
        )

    def last_arrival(j, n):
        to = lax.rem(chip + j, z.chips)
        return remote(
            v.last_out.at[to, n], v.last_in.at[to, n], v.last_send.at[j, n], v.last_recv.at[to, n], {"pool": 2 * to + core}
        )

    for n in range(z.parts):

        @pl.loop(0, z.part // z.out_tile)
        def _(m):
            down(z.groups - 1, pl.ds(pl.multiple_of(n * z.part + m * z.out_tile, 128), z.out_tile))

        v.end_out[n] = v.acc[other, pl.ds(n * z.part, z.part)].astype(bf16)
        end_copy(n).start()
    for j in range(1, z.pools):
        for k in range(CHUNKS):
            att_copy(j, k).wait_send()
    for n in range(z.parts):
        pair_copy(n).wait_send()
        in_copy(n).wait_send()
        for j in range(1, z.chips):
            chip_copy(j, n).wait_send()
    sq_copy.wait_send()
    for s in range(2):

        @pl.when(t != ends[s])
        def _():
            square_copy(s).wait_send()

    @pl.loop(0, CHUNKS)
    def _(k):
        for origin in range(z.tps):

            @pl.when((t < last) & (origin <= t))
            def _():
                slab_right(origin, k).wait_send()

            @pl.when((t > 0) & (origin >= t))
            def _():
                slab_left(origin, k).wait_send()

    for n in range(z.parts):
        at = pl.ds(n * z.part, z.part)
        end_copy(n).wait_recv()
        v.post[:, at] = v.acc[mine, at] + v.end_in[n].astype(f32)
        for q in range(z.chips):
            v.last_out[q, n] = v.post[pl.ds(q * z.block, z.block), at].astype(bf16)
        for j in range(1, z.chips):
            last_copy(j, n).start()
    @pl.loop(0, z.pieces)
    def _(c):
        for s in range(2):
            far, _, _ = lanes(s)

            @pl.when(far < last)
            def _():
                sum_hop(s, c).wait_send()

            @pl.when((far > 0) & (c < z.groups))
            def _():
                hidden_hop(s, c).wait_send()
    for n in range(z.parts):
        at = pl.ds(n * z.part, z.part)
        total = v.own_post[:, at] + v.post[block_in_half, at]
        for j in range(1, z.chips):
            last_arrival(j, n).wait_recv()
            total = total + v.last_in[lax.rem(chip + j, z.chips), n].astype(f32)
        out[:, at] = total.astype(bf16)

    for n in range(z.parts):
        end_copy(n).wait_send()
        for j in range(1, z.chips):
            last_copy(j, n).wait_send()


def on_device(
    queries,
    cached_entries,
    new_entry,
    lengths,
    residual,
    out_weight,
    norm_gain,
    gate_weight,
    up_weight,
    down_weight,
):
    pools, tps = lax.axis_size("pool"), lax.axis_size("tp")
    amount, cols = queries.shape[0], queries.shape[1] // pools
    block, width = residual.shape
    z = sizes_of(pools, tps, amount, cached_entries.shape[1], block, width, cols, gate_weight.shape[1])

    local = np.arange(z.slab)
    pick_local = np.zeros((z.slab, pools * PAD), np.float32)
    pick_local[local, local // amount * PAD + local % amount] = 1
    every = np.arange(z.rows)
    of_core, of_chip = every // z.half, every % z.half // block
    of_tp, of_row = every // amount % tps, every % amount
    pick_all = np.zeros((z.rows, z.rows), np.float32)
    pick_all[every, (of_tp * pools + 2 * of_chip + of_core) * amount + of_row] = 1

    vmem = pl.BlockSpec(memory_space=pltpu.VMEM)
    anywhere = pl.BlockSpec(memory_space=pl.ANY)
    bf16 = jnp.bfloat16
    held = scratch_of(z)
    return pl.pallas_call(
        functools.partial(layer_kernel, z, tuple(held)),
        out_shape=jax.ShapeDtypeStruct((block, width), bf16),
        in_specs=[pl.BlockSpec(memory_space=pltpu.SMEM), vmem] + [anywhere] * 10,
        out_specs=vmem,
        scratch_shapes=list(held.values()),
        compiler_params=pltpu.CompilerParams(
            collective_id=0, has_side_effects=True, vmem_limit_bytes=62 << 20
        ),
        name="layer",
    )(
        lengths,
        new_entry,
        queries,
        residual,
        norm_gain,
        jnp.asarray(pick_local, bf16),
        jnp.asarray(pick_all, bf16),
        cached_entries,
        out_weight,
        gate_weight,
        up_weight,
        down_weight,
    )


def solution(mesh):
    placed = (
        P(("groups", "pool", "tp"), None),
        P(("groups", "pool", "tp"), None, None),
        P(("groups", "pool", "tp"), None),
        P(("groups", "pool", "tp")),
        P(("groups", "pool"), "tp"),
        P("pool", "tp"),
        P("tp"),
        P("tp", "pool"),
        P("tp", "pool"),
        P("pool", "tp"),
    )
    return jax.shard_map(
        on_device,
        mesh=mesh,
        in_specs=placed,
        out_specs=P(("groups", "pool"), "tp"),
        check_vma=False,
    )
```
